256 devices in a mesh: gx: 4 (over x), gy: 16 (over z_lo, y), gz: 4 (over z_hi, core).
Axes of the slice: x: 4, y: 4, z: 8 (z_hi: 2, z_lo: 4; z = z_hi * 4 + z_lo), core: 2. Of those that a mesh axis runs over, the one named last changes fastest.
Arguments:
- species: int32 [4, 16, 4, 256], P('gx', 'gy', 'gz'), may hold values from 0 to 7
- neighbour_index: int32 [4, 16, 4, 32, 256], P('gx', 'gy', 'gz'), may hold values from 0 to 639
- neighbour_count: int32 [4, 16, 4, 256], P('gx', 'gy', 'gz'), may hold values from 16 to 32, as said below
- edge_vectors: float32 [4, 16, 4, 3, 32, 256], P('gx', 'gy', 'gz'), as said below
- ghost_send: int32 [4, 16, 4, 3, 128], P('gx', 'gy', 'gz'), may hold values from 0 to 511, as said below
- brick_send: int32 [4, 16, 4, 512], P('gx', 'gy', 'gz'), may hold values from 0 to 639
- probe_index: int32 [4, 16, 4, 32, 512], P('gx', 'gy', 'gz'), may hold values from 0 to 511, as said below
- probe_count: int32 [4, 16, 4, 512], P('gx', 'gy', 'gz'), may hold values from 8 to 32, as said below
- probe_vectors: float32 [4, 16, 4, 3, 32, 512], P('gx', 'gy', 'gz'), as said below
- embedding: bfloat16 [8, 128], replicated, may hold values from -4 to 4
- message_one: bfloat16 [128, 128], replicated, may hold values from -0.5 to 0.5
- radial_in_one: bfloat16 [8, 64], replicated, may hold values from -2 to 2
- radial_out_one: bfloat16 [64, 512], replicated, may hold values from -0.75 to 0.75
- self_mix: bfloat16 [128, 128], replicated, may hold values from -0.5 to 0.5
- basis_mix: bfloat16 [512, 128], replicated, may hold values from -0.25 to 0.25
- message_two: bfloat16 [128, 128], replicated, may hold values from -0.5 to 0.5
- radial_in_two: bfloat16 [8, 64], replicated, may hold values from -2 to 2
- radial_out_two: bfloat16 [64, 512], replicated, may hold values from -0.75 to 0.75
- decoder: bfloat16 [4, 128, 8], replicated, may hold values from -0.5 to 0.5
Outputs:
- density: float32 [4, 16, 4, 512], P('gx', 'gy', 'gz')
The draws below stay inside these ranges and needn't reach their ends.
Inputs may be any that keep to these rules, and one draw needn't show every extreme that they name: `neighbour_count`: each domain has an atom with all 32 slots live. `edge_vectors`: lengths lie between 0.8 and 5. `ghost_send`: section s entries index the first 256 + 2 s * 64 rows of the table. `probe_index`: an entry s * 32 + t refers to source s of the gy column, which lies at most 2 domains from the brick along gy (periodically); for each source and brick only t below a fixed live count (at least 16, all 32 from the brick's own domain) occurs. `probe_count`: each brick has a probe with all 32 slots live. `probe_vectors`: lengths lie between 0.5 and 4.
All inputs are finite; a program needn't handle non-finite values.
Results may differ from the reference program's by a relative error of at most 0.0064.
Values may be sent and summed in bfloat16 or wider, within the bound.
No kernel may reach another device: no remote copies, remote signals or barrier semaphores. Data moves between devices by JAX's collectives and lax.ppermute only.
A program may use at most 128 MiB of HBM per device.

```python
import math
import jax
import jax.numpy as jnp
from jax import lax

CHANNELS = 128
BASIS = 8
RADIAL_HIDDEN = 64
SPECIES = 8
NEIGHBOURS = 32
PROBE_NEIGHBOURS = 32
ATOMS_DEV = 256
PROBES_DEV = 512
GHOSTS = 64
CAPACITY = 32
TABLE = 640
N_GX = 4
N_GY = 16
N_GZ = 4


def random_vectors(key, shape, low, high):
    keys = jax.random.split(key, 3)
    radius = jax.random.uniform(keys[0], shape, jnp.float32, low, high)
    cosine = jax.random.uniform(keys[1], shape, jnp.float32, -1.0, 1.0)
    azimuth = jax.random.uniform(keys[2], shape, jnp.float32, -math.pi, math.pi)
    sine = jnp.sqrt(jnp.maximum(1.0 - cosine * cosine, 0.0))
    return jnp.stack([radius * sine * jnp.cos(azimuth), radius * sine * jnp.sin(azimuth), radius * cosine], axis=3)


def draw_neighbour_count(key, part):
    counts = jax.random.randint(key, (N_GX, N_GY, N_GZ, ATOMS_DEV), NEIGHBOURS // 2, NEIGHBOURS + 1)
    return counts.at[..., 0].set(NEIGHBOURS).astype(jnp.int32)


def draw_edge_vectors(key, part):
    shape = (N_GX, N_GY, N_GZ, NEIGHBOURS, ATOMS_DEV)
    return random_vectors(key, shape, 0.8, 4.9)


def draw_ghost_send(key, part):
    keys = jax.random.split(key, 3)
    pieces = []
    for section_index in range(3):
        pieces.append(jax.random.randint(keys[section_index], (N_GX, N_GY, N_GZ, 1, 2 * GHOSTS), 0, ATOMS_DEV + 2 * GHOSTS * section_index))
    return jnp.concatenate(pieces, axis=3).astype(jnp.int32)


def draw_probe_index(key, part):
    live_counts = jax.random.randint(jax.random.fold_in(key, 11), (N_GX, N_GY, N_GZ, N_GY), CAPACITY // 2, CAPACITY + 1)
    own_brick = lax.broadcasted_iota(jnp.int32, (N_GX, N_GY, N_GZ, N_GY), 1) == lax.broadcasted_iota(jnp.int32, (N_GX, N_GY, N_GZ, N_GY), 3)
    live_counts = jnp.where(own_brick, CAPACITY, live_counts)
    shape = (N_GX, N_GY, N_GZ, PROBE_NEIGHBOURS, PROBES_DEV)
    index_x = lax.broadcasted_iota(jnp.int32, shape, 0)
    index_y = lax.broadcasted_iota(jnp.int32, shape, 1)
    index_z = lax.broadcasted_iota(jnp.int32, shape, 2)
    step = jax.random.randint(jax.random.fold_in(key, 12), shape, -2, 3)
    source = (index_y + step + 2 * N_GY) % N_GY
    offset = jax.random.randint(jax.random.fold_in(key, 13), shape, 0, 1048576)
    bound = live_counts[index_x, source, index_z, index_y]
    return (source * CAPACITY + offset % bound).astype(jnp.int32)


def draw_probe_count(key, part):
    counts = jax.random.randint(key, (N_GX, N_GY, N_GZ, PROBES_DEV), PROBE_NEIGHBOURS // 4, PROBE_NEIGHBOURS + 1)
    return counts.at[..., 0].set(PROBE_NEIGHBOURS).astype(jnp.int32)


def draw_probe_vectors(key, part):
    shape = (N_GX, N_GY, N_GZ, PROBE_NEIGHBOURS, PROBES_DEV)
    return random_vectors(key, shape, 0.5, 3.9)


def place_ends(values, key, least, top_value):
    extent = values.shape
    spot = [jax.random.randint(jax.random.fold_in(key, axis), (), 0, extent[axis]) for axis in range(len(extent))]
    values = values.at[tuple(spot)].set(least)
    longest = extent.index(max(extent))
    spot[longest] = (spot[longest] + 1) % extent[longest]
    return values.at[tuple(spot)].set(top_value)


def gaussian(key, shape, scale, most, held_as=jnp.bfloat16):
    return jnp.clip(scale * jax.random.normal(key, shape, jnp.float32), -most, most).astype(held_as)


def setup_inputs(seed: int = 0) -> dict:
    key_of = jax.random.split(jax.random.key(seed), 20)
    species = place_ends(jax.random.randint(key_of[0], (N_GX, N_GY, N_GZ, ATOMS_DEV), 0, SPECIES), jax.random.fold_in(key_of[0], 1), 0, SPECIES - 1).astype(jnp.int32)
    neighbour_index = place_ends(jax.random.randint(key_of[1], (N_GX, N_GY, N_GZ, NEIGHBOURS, ATOMS_DEV), 0, TABLE), jax.random.fold_in(key_of[1], 1), 0, TABLE - 1).astype(jnp.int32)
    neighbour_count = draw_neighbour_count(jax.random.fold_in(key_of[19], 71), 0)
    edge_vectors = draw_edge_vectors(jax.random.fold_in(key_of[19], 71), 0)
    ghost_send = draw_ghost_send(jax.random.fold_in(key_of[19], 71), 0)
    brick_send = place_ends(jax.random.randint(key_of[5], (N_GX, N_GY, N_GZ, N_GY * CAPACITY), 0, TABLE), jax.random.fold_in(key_of[5], 1), 0, TABLE - 1).astype(jnp.int32)
    probe_index = draw_probe_index(jax.random.fold_in(key_of[19], 71), 0)
    probe_count = draw_probe_count(jax.random.fold_in(key_of[19], 71), 0)
    probe_vectors = draw_probe_vectors(jax.random.fold_in(key_of[19], 71), 0)
    embedding = gaussian(key_of[9], (SPECIES, CHANNELS), 1.0, 4.0)
    message_one = gaussian(key_of[10], (CHANNELS, CHANNELS), CHANNELS ** -0.5, 0.5)
    radial_in_one = gaussian(key_of[11], (BASIS, RADIAL_HIDDEN), BASIS ** -0.5, 2.0)
    radial_out_one = gaussian(key_of[12], (RADIAL_HIDDEN, 4 * CHANNELS), RADIAL_HIDDEN ** -0.5, 0.75)
    self_mix = gaussian(key_of[13], (CHANNELS, CHANNELS), CHANNELS ** -0.5, 0.5)
    basis_mix = gaussian(key_of[14], (4 * CHANNELS, CHANNELS), (4 * CHANNELS) ** -0.5, 0.25)
    message_two = gaussian(key_of[15], (CHANNELS, CHANNELS), CHANNELS ** -0.5, 0.5)
    radial_in_two = gaussian(key_of[16], (BASIS, RADIAL_HIDDEN), BASIS ** -0.5, 2.0)
    radial_out_two = gaussian(key_of[17], (RADIAL_HIDDEN, 4 * CHANNELS), RADIAL_HIDDEN ** -0.5, 0.75)
    decoder = gaussian(key_of[18], (4, CHANNELS, BASIS), CHANNELS ** -0.5, 0.5)
    return {"species": species, "neighbour_index": neighbour_index, "neighbour_count": neighbour_count, "edge_vectors": edge_vectors, "ghost_send": ghost_send, "brick_send": brick_send, "probe_index": probe_index, "probe_count": probe_count, "probe_vectors": probe_vectors, "embedding": embedding, "message_one": message_one, "radial_in_one": radial_in_one, "radial_out_one": radial_out_one, "self_mix": self_mix, "basis_mix": basis_mix, "message_two": message_two, "radial_in_two": radial_in_two, "radial_out_two": radial_out_two, "decoder": decoder}


def harmonics(vectors):
    radius = jnp.sqrt(vectors[0] * vectors[0] + vectors[1] * vectors[1] + vectors[2] * vectors[2])
    along_x = vectors[0] / radius
    along_y = vectors[1] / radius
    along_z = vectors[2] / radius
    ones_row = jnp.ones_like(radius)
    root_three = math.sqrt(3.0)
    root_fifteen = math.sqrt(15.0)
    root_five = math.sqrt(5.0)
    root_hundred = math.sqrt(105.0)
    root_seven = math.sqrt(7.0)
    outer_coef = math.sqrt(35.0 / 8.0)
    inner_coef = math.sqrt(21.0 / 8.0)
    rows_list = [ones_row, root_three * along_x, root_three * along_y, root_three * along_z, root_fifteen * along_x * along_y, root_fifteen * along_y * along_z, 0.5 * root_five * (3.0 * along_z * along_z - 1.0), root_fifteen * along_x * along_z, 0.5 * root_fifteen * (along_x * along_x - along_y * along_y), outer_coef * along_y * (3.0 * along_x * along_x - along_y * along_y), root_hundred * along_x * along_y * along_z, inner_coef * along_y * (5.0 * along_z * along_z - 1.0), 0.5 * root_seven * along_z * (5.0 * along_z * along_z - 3.0), inner_coef * along_x * (5.0 * along_z * along_z - 1.0), 0.5 * root_hundred * along_z * (along_x * along_x - along_y * along_y), outer_coef * along_x * (along_x * along_x - 3.0 * along_y * along_y)]
    return (jnp.stack(rows_list), radius)

def radial_basis(radius, cutoff):
    scaled = radius / cutoff
    envelope = 1.0 - 28.0 * scaled ** 6 + 48.0 * scaled ** 7 - 21.0 * scaled ** 8
    order_grid = jnp.arange(1, BASIS + 1).astype(jnp.float32).reshape((BASIS,) + (1,) * radius.ndim)
    return math.sqrt(2.0 / cutoff) * jnp.sin(order_grid * (math.pi / cutoff) * radius[None]) / radius[None] * envelope[None]

def layer_sums(ghost_table, slot_index, slot_count, vector_set, radial_in, radial_out):
    neigh_slots, atom_rows = slot_index.shape
    channels = ghost_table.shape[1]
    block_rows = 128 if atom_rows % 128 == 0 else atom_rows
    slot_ids = lax.iota(jnp.int32, neigh_slots)

    def one_block(first_row):
        index_block = lax.dynamic_slice_in_dim(slot_index, first_row, block_rows, 1)
        count_block = lax.dynamic_slice_in_dim(slot_count, first_row, block_rows, 0)
        vector_block = lax.dynamic_slice_in_dim(vector_set, first_row, block_rows, 2)
        angular, radius = harmonics(vector_block)
        radial_values = radial_basis(radius, 5.0).astype(jnp.bfloat16)
        hidden = jax.nn.silu(jnp.einsum('nkb,nh->kbh', radial_values.astype(jnp.float32), radial_in.astype(jnp.float32), precision=lax.Precision.HIGHEST)).astype(jnp.bfloat16)
        radial = jnp.einsum('kbh,hf->kbf', hidden.astype(jnp.float32), radial_out.astype(jnp.float32), precision=lax.Precision.HIGHEST)
        live_mask = (slot_ids[:, None] < count_block[None, :]).astype(jnp.float32)
        picked = jnp.take(ghost_table, index_block, axis=0).astype(jnp.float32) * live_mask[:, :, None]
        pieces = []
        for degree in range(4):
            weighted = radial[:, :, degree * channels:(degree + 1) * channels] * picked
            pieces.append(jnp.einsum('mkb,kbc->bmc', angular[degree * degree:(degree + 1) * (degree + 1)], weighted, precision=lax.Precision.HIGHEST))
        return 0.25 * jnp.concatenate(pieces, axis=1)
    starts = (jnp.arange(atom_rows // block_rows) * block_rows).astype(jnp.int32)
    return lax.map(one_block, starts).reshape(atom_rows, 16, channels)

def node_update(previous, sums, self_mix, basis_mix):
    pieces = [sums[:, 0, :]]
    for degree in (1, 2, 3):
        pieces.append(lax.optimization_barrier(jnp.sum(sums[:, degree * degree:(degree + 1) * (degree + 1), :] ** 2, axis=1)))
    mixed_in = jnp.concatenate(pieces, axis=1).astype(jnp.bfloat16)
    summed = jnp.dot(previous, self_mix, preferred_element_type=jnp.float32) + jnp.dot(mixed_in, basis_mix, preferred_element_type=jnp.float32)
    return jax.nn.silu(summed).astype(jnp.bfloat16)

def coefficients(features, decoder):
    row_count = features.shape[0]
    pieces = []
    for degree in range(4):
        part_rows = features[:, degree * degree:(degree + 1) * (degree + 1), :].astype(jnp.float32)
        pieces.append(jnp.einsum('rmc,cn->rmn', part_rows, decoder[degree].astype(jnp.float32), precision=lax.Precision.HIGHEST))
    return jnp.concatenate(pieces, axis=1).astype(jnp.bfloat16).reshape(row_count, -1)

def density_of(received, slot_index, slot_count, vector_set):
    probe_slots, probe_rows = slot_index.shape
    block_rows = 512 if probe_rows % 512 == 0 else probe_rows
    slot_ids = lax.iota(jnp.int32, probe_slots)

    def one_block(first_row):
        index_block = lax.dynamic_slice_in_dim(slot_index, first_row, block_rows, 1)
        count_block = lax.dynamic_slice_in_dim(slot_count, first_row, block_rows, 0)
        vector_block = lax.dynamic_slice_in_dim(vector_set, first_row, block_rows, 2)
        angular, radius = harmonics(vector_block)
        radial_values = radial_basis(radius, 4.0)
        outer_basis = (angular.transpose(1, 2, 0)[:, :, :, None] * radial_values.transpose(1, 2, 0)[:, :, None, :]).reshape(probe_slots, block_rows, -1)
        picked = jnp.take(received, index_block, axis=0).astype(jnp.float32)
        live_mask = (slot_ids[:, None] < count_block[None, :]).astype(jnp.float32)
        return 0.125 * lax.optimization_barrier(jnp.sum(lax.optimization_barrier(jnp.sum(outer_basis * picked, axis=2)) * live_mask, axis=0))
    starts = (jnp.arange(probe_rows // block_rows) * block_rows).astype(jnp.int32)
    return lax.map(one_block, starts).reshape(probe_rows)

def grid_extend(row_grid, send_lists):
    ghost_rows = send_lists.shape[-1] // 2
    ghost_table = row_grid
    for section_index in range(3):
        chosen = jnp.take_along_axis(ghost_table, send_lists[:, :, :, section_index, :, None], axis=3)
        from_lower = jnp.roll(chosen, 1, axis=section_index)[:, :, :, ghost_rows:, :]
        from_higher = jnp.roll(chosen, -1, axis=section_index)[:, :, :, :ghost_rows, :]
        ghost_table = jnp.concatenate([ghost_table, from_lower, from_higher], axis=3)
    return ghost_table

def reference(species, neighbour_index, neighbour_count, edge_vectors, ghost_send, brick_send, probe_index, probe_count, probe_vectors, embedding, message_one, radial_in_one, radial_out_one, self_mix, basis_mix, message_two, radial_in_two, radial_out_two, decoder):
    grid_shape = (N_GX, N_GY, N_GZ)
    devices = N_GX * N_GY * N_GZ
    atom_rows = species.shape[-1]
    channels = embedding.shape[1]
    onehot = (species.reshape(-1)[:, None] == lax.iota(jnp.int32, embedding.shape[0])[None, :]).astype(jnp.float32)
    start_h = jnp.dot(onehot, embedding.astype(jnp.float32), precision=lax.Precision.HIGHEST).astype(jnp.bfloat16)

    def run_layer(tables, radial_in, radial_out):
        item_set = (tables.reshape((devices,) + tables.shape[3:]), neighbour_index.reshape((devices,) + neighbour_index.shape[3:]), neighbour_count.reshape(devices, atom_rows), edge_vectors.reshape((devices,) + edge_vectors.shape[3:]))
        sums = lax.map(lambda item_one: layer_sums(item_one[0], item_one[1], item_one[2], item_one[3], radial_in, radial_out), item_set)
        return sums.reshape(devices * atom_rows, 16, channels)
    first_msg = jnp.dot(start_h, message_one, preferred_element_type=jnp.float32).astype(jnp.bfloat16)
    sums_one = run_layer(grid_extend(first_msg.reshape(grid_shape + (atom_rows, channels)), ghost_send), radial_in_one, radial_out_one)
    next_h = node_update(start_h, sums_one, self_mix, basis_mix)
    second_msg = jnp.dot(next_h, message_two, preferred_element_type=jnp.float32).astype(jnp.bfloat16)
    features = run_layer(grid_extend(second_msg.reshape(grid_shape + (atom_rows, channels)), ghost_send), radial_in_two, radial_out_two).astype(jnp.bfloat16)
    coeff_rows = coefficients(features, decoder)
    coeff_table = grid_extend(coeff_rows.reshape(grid_shape + (atom_rows, -1)), ghost_send)
    chosen = jnp.take_along_axis(coeff_table, brick_send[..., None], axis=3)
    capacity = brick_send.shape[-1] // N_GY
    chosen = chosen.reshape(N_GX, N_GY, N_GZ, N_GY, capacity, -1).transpose(0, 3, 2, 1, 4, 5).reshape(devices, N_GY * capacity, -1)
    item_set = (chosen, probe_index.reshape((devices,) + probe_index.shape[3:]), probe_count.reshape(devices, -1), probe_vectors.reshape((devices,) + probe_vectors.shape[3:]))
    result = lax.map(lambda item_one: density_of(item_one[0], item_one[1], item_one[2], item_one[3]), item_set)
    return result.reshape(N_GX, N_GY, N_GZ, -1)
```

```python
import math

import jax
import jax.numpy as jnp
from jax import lax
from jax.experimental import pallas as pl
from jax.experimental.pallas import tpu as pltpu
from jax.sharding import PartitionSpec as P

BASIS = 8
F32 = jnp.float32
BF16 = jnp.bfloat16
VMEM = pl.BlockSpec(memory_space=pltpu.VMEM)
SMEM = pl.BlockSpec(memory_space=pltpu.SMEM)


def call(kernel, out_shape, operands, scratch=(), flops=0, moved=1 << 20, specs=None):
    many = isinstance(out_shape, (list, tuple))
    return pl.pallas_call(
        kernel,
        out_shape=out_shape,
        in_specs=specs or [VMEM] * len(operands),
        out_specs=[VMEM] * len(out_shape) if many else VMEM,
        scratch_shapes=list(scratch),
        cost_estimate=pl.CostEstimate(flops=flops, bytes_accessed=moved, transcendentals=0),
    )(*operands)


def dot(a, b):
    return jnp.dot(a, b, preferred_element_type=F32)


def dot_first(a, b):
    return lax.dot_general(a, b, (((0,), (0,)), ((), ())), preferred_element_type=F32)


def harmonics(vx, vy, vz, weight):
    radius = jnp.sqrt(vx * vx + vy * vy + vz * vz)
    inverse = 1.0 / radius
    x, y, z = vx * inverse, vy * inverse, vz * inverse
    xx, yy, zz = x * x, y * y, z * z
    r3, r15, r5, r105, r7 = (math.sqrt(v) for v in (3.0, 15.0, 5.0, 105.0, 7.0))
    outer, inner = math.sqrt(35.0 / 8.0), math.sqrt(21.0 / 8.0)
    rows = [
        jnp.ones_like(x),
        r3 * x,
        r3 * y,
        r3 * z,
        r15 * x * y,
        r15 * y * z,
        0.5 * r5 * (3.0 * zz - 1.0),
        r15 * x * z,
        0.5 * r15 * (xx - yy),
        outer * y * (3.0 * xx - yy),
        r105 * x * y * z,
        inner * y * (5.0 * zz - 1.0),
        0.5 * r7 * z * (5.0 * zz - 3.0),
        inner * x * (5.0 * zz - 1.0),
        0.5 * r105 * z * (xx - yy),
        outer * x * (xx - 3.0 * yy),
    ]
    return [row * weight for row in rows], radius, inverse


def radial_basis(radius, inverse, cutoff):
    u = radius * (1.0 / cutoff)
    u2 = u * u
    envelope = 1.0 + u2 * u2 * u2 * (-28.0 + u * (48.0 - 21.0 * u))
    scale = math.sqrt(2.0 / cutoff) * inverse * envelope
    angle = radius * (math.pi / cutoff)
    before, now = jnp.zeros_like(angle), jnp.sin(angle)
    twice = 2.0 * jnp.cos(angle)
    rows = []
    for _ in range(BASIS):
        rows.append(now * scale)
        before, now = now, twice * now - before
    return rows


def sections(arrays):
    return jnp.where(lax.broadcasted_iota(jnp.int32, (8, 128), 1) < 64, arrays[1], arrays[0])


def swapped(index):
    return jnp.where(index >= 256, index ^ 64, index)


def species_rows(species_ref, pieces):
    parts = [jnp.broadcast_to(species_ref[...].astype(F32), (8, 256))]
    for first in range(0, len(pieces), 2):
        parts.append(sections((pieces[first][...], pieces[first + 1][...])))
    return jnp.concatenate(parts, axis=1)


def pick_species(section):
    def kernel(species_ref, lists_ref, *rest):
        out_ref = rest[-1]
        table = species_rows(species_ref, rest[:-1]).astype(BF16)
        rows = table.shape[1]
        chosen = swapped(lists_ref[section : section + 1, :])
        onehot = lax.broadcasted_iota(jnp.int32, (rows, 128), 0) == chosen
        out_ref[...] = dot(table, jnp.where(onehot, 1.0, 0.0).astype(BF16))

    return kernel


def store_rows(ref, rows):
    for n, row in enumerate(rows):
        size = row.shape[0]
        for tile in range(ref.shape[0]):
            ref[tile, n * size : (n + 1) * size, :] = row[:, tile * 128 : (tile + 1) * 128]


def spread(ref, row):
    parts = [ref[tile, pl.ds(row, 8, stride=0), :] for tile in range(ref.shape[0])]
    return jnp.concatenate(parts, axis=1)


def basis_rows(ref, slot, slots):
    parts = [ref[tile, pl.ds(slot, BASIS, stride=slots), :] for tile in range(ref.shape[0])]
    return jnp.concatenate(parts, axis=1)


def geometry_kernel(vec_ref, count_ref, in1_ref, in2_ref, y_ref, hid1_ref, hid2_ref, phi):
    slots, atoms = vec_ref.shape[1:]
    live = lax.broadcasted_iota(jnp.int32, (slots, atoms), 0) < count_ref[...]
    weight = jnp.where(live, 0.25, 0.0)
    rows, radius, inverse = harmonics(vec_ref[0], vec_ref[1], vec_ref[2], weight)
    store_rows(y_ref, rows)
    store_rows(phi, radial_basis(radius, inverse, 5.0))
    into1 = in1_ref[...].astype(F32).T.astype(BF16)
    into2 = in2_ref[...].astype(F32).T.astype(BF16)
    for k in range(slots):
        basis = basis_rows(phi, k, slots).astype(BF16)
        for into, out in ((into1, hid1_ref), (into2, hid2_ref)):
            value = dot(into, basis)
            out[k] = (value / (1.0 + jnp.exp(-value))).astype(BF16)


def slot_sums(weighted, y_ref, finish):
    slots, _, atoms = weighted.shape
    tiles = atoms // 128

    def block(j, carry):
        first = pl.multiple_of((j // tiles) * 16, 16)
        tile = j % tiles
        lane = pl.multiple_of(tile * 128, 128)
        sums = [[jnp.zeros((8, 128), F32) for _ in range(16)] for _ in range(2)]
        for k in range(slots):
            for degree in range(4):
                w = [
                    weighted[k, pl.ds(degree * 128 + first + 8 * h, 8), pl.ds(lane, 128)]
                    for h in range(2)
                ]
                for m in range(degree * degree, (degree + 1) * (degree + 1)):
                    y = y_ref[tile, pl.ds(m * slots + k, 8, stride=0), :]
                    for h in range(2):
                        sums[h][m] = sums[h][m] + y * w[h]
        finish(first, lane, [jnp.concatenate([sums[0][m], sums[1][m]], axis=0) for m in range(16)])
        return carry

    lax.fori_loop(0, 8 * tiles, block, 0)


def layer_one_kernel(
    species_ref, xl, xh, yl, yh, zl, zh, index_ref, y_ref, hid_ref, out_ref, emb_ref, msg1_ref,
    self_ref, mix_ref, msg2_ref, next_ref, weighted, kinds, feats,
):
    slots, atoms = index_ref.shape
    table = species_rows(species_ref, (xl, xh, yl, yh, zl, zh))
    for row in range(0, slots, 8):
        for lane in range(0, atoms, 128):
            where = swapped(index_ref[row : row + 8, lane : lane + 128])
            found = jnp.zeros((8, 128), F32)
            for b in range(5):
                part = jnp.take_along_axis(table[:, b * 128 : (b + 1) * 128], where & 127, axis=1)
                found = jnp.where((where >> 7) == b, part, found)
            kinds[lane // 128, row : row + 8, :] = found
    rows = dot(emb_ref[...], msg1_ref[...]).astype(BF16).astype(F32)
    rows_t = rows.T.astype(BF16)
    out_t = out_ref[...].astype(F32).T.astype(BF16)
    kind_ids = lax.broadcasted_iota(jnp.int32, (8, atoms), 0).astype(F32)

    def fill(k, carry):
        radial = dot(out_t, hid_ref[k])
        onehot = jnp.where(spread(kinds, k) == kind_ids, 1.0, 0.0).astype(BF16)
        picked = dot(rows_t, onehot)
        for degree in range(4):
            weighted[k, degree * 128 : (degree + 1) * 128, :] = (
                radial[degree * 128 : (degree + 1) * 128] * picked
            )
        return carry

    lax.fori_loop(0, slots, fill, 0)

    def finish(first, lane, sums):
        feats[pl.ds(first, 16), pl.ds(lane, 128)] = sums[0].astype(BF16)
        for degree in (1, 2, 3):
            total = sums[degree * degree] * sums[degree * degree]
            for m in range(degree * degree + 1, (degree + 1) * (degree + 1)):
                total = total + sums[m] * sums[m]
            feats[pl.ds(degree * 128 + first, 16), pl.ds(lane, 128)] = total.astype(BF16)

    slot_sums(weighted, y_ref, finish)
    own = jnp.where(table[:, :atoms] == kind_ids, 1.0, 0.0).astype(BF16)
    start = dot_first(emb_ref[...].astype(F32), own.astype(F32)).astype(BF16)
    mixed = dot_first(self_ref[...], start) + dot_first(mix_ref[...], feats[...])
    hidden = (mixed / (1.0 + jnp.exp(-mixed))).astype(BF16)
    next_ref[...] = dot_first(hidden, msg2_ref[...]).astype(BF16)


def layer_two_kernel(
    own_ref, xl, xh, yl, yh, zl, zh, index_ref, y_ref, hid_ref, out_ref, dec_ref, coeff_ref,
    weighted, feats, table,
):
    slots, atoms = index_ref.shape
    table[:atoms, :] = own_ref[...].astype(F32)
    for n, piece in enumerate((xl, xh, yl, yh, zl, zh)):
        table[atoms + 64 * n : atoms + 64 * (n + 1), :] = piece[...].astype(F32)
    rows = table.shape[0]
    rows_t = table[...].T.astype(BF16)
    out_t = out_ref[...].astype(F32).T.astype(BF16)
    row_ids = lax.broadcasted_iota(jnp.int32, (rows, atoms), 0)

    def fill(k, carry):
        radial = dot(out_t, hid_ref[k])
        onehot = jnp.where(index_ref[pl.ds(k, 1), :] == row_ids, 1.0, 0.0).astype(BF16)
        picked = dot(rows_t, onehot)
        for degree in range(4):
            weighted[k, degree * 128 : (degree + 1) * 128, :] = (
                radial[degree * 128 : (degree + 1) * 128] * picked
            )
        return carry

    lax.fori_loop(0, slots, fill, 0)

    def finish(first, lane, sums):
        for m in range(16):
            feats[pl.ds(m * 128 + first, 16), pl.ds(lane, 128)] = sums[m].astype(BF16)

    slot_sums(weighted, y_ref, finish)
    group = lax.broadcasted_iota(jnp.int32, (128, 128), 0) >> 3
    total = jnp.zeros((128, atoms), F32)
    for degree in range(4):
        tall = jnp.concatenate([dec_ref[degree].astype(F32).T] * 16, axis=0)
        for m in range(degree * degree, (degree + 1) * (degree + 1)):
            part = jnp.where(group == m, tall, 0.0).astype(BF16)
            total = total + dot(part, feats[m * 128 : (m + 1) * 128, :])
    coeff_ref[...] = total.T.astype(BF16)


def density_kernel(
    here_ref, p0, p1, p2, p3, p4, index_ref, count_ref, vec_ref, out_ref, y, phi, table
):
    slots, probes = index_ref.shape
    live = lax.broadcasted_iota(jnp.int32, (slots, probes), 0) < count_ref[...]
    weight = jnp.where(live, 0.125, 0.0)
    rows, radius, inverse = harmonics(vec_ref[0], vec_ref[1], vec_ref[2], weight)
    store_rows(y, rows)
    store_rows(phi, radial_basis(radius, inverse, 4.0))
    table[...] = jnp.zeros_like(table)
    for n, piece in enumerate((p0, p1, p2, p3, p4)):
        table[32 * n : 32 * (n + 1), :] = piece[...].astype(F32)
    rows_t = table[...].T.astype(BF16)
    row_ids = lax.broadcasted_iota(jnp.int32, (table.shape[0], probes), 0)
    column, here = here_ref[1], here_ref[0]

    def slot(k, total):
        index = index_ref[pl.ds(k, 1), :]
        source = (index >> 5) - here + 2
        source = jnp.where(source < 0, source + column, source)
        source = jnp.where(source >= column, source - column, source)
        where = source * 32 + (index & 31)
        onehot = jnp.where(where == row_ids, 1.0, 0.0).astype(BF16)
        picked = dot(rows_t, onehot)
        part = jnp.zeros((8, probes), F32)
        for m in range(16):
            part = part + spread(y, m * slots + k) * picked[m * 8 : (m + 1) * 8]
        return total + part * basis_rows(phi, k, slots)

    total = lax.fori_loop(0, slots, slot, jnp.zeros((8, probes), F32))
    out_ref[...] = jnp.sum(total, axis=0, keepdims=True)


def shifted(block, axis, step):
    size = lax.axis_size(axis)
    return lax.ppermute(block, axis, [(i, (i + step) % size) for i in range(size)])


def extend(rows, lists):
    table = rows
    pieces = []
    for section, axis in enumerate(("gx", "gy", "gz")):
        chosen = jnp.take(table, lists[section], axis=0)
        low = shifted(chosen[64:], axis, 1)
        high = shifted(chosen[:64], axis, -1)
        pieces += [low, high]
        if section < 2:
            table = jnp.concatenate([table, low, high], axis=0)
    return pieces


def shards(
    species, neighbour_index, neighbour_count, edge_vectors, ghost_send, brick_send, probe_index,
    probe_count, probe_vectors, embedding, message_one, radial_in_one, radial_out_one, self_mix,
    basis_mix, message_two, radial_in_two, radial_out_two, decoder,
):
    slots, atoms = neighbour_index.shape[3:]
    probes = probe_index.shape[-1]
    kinds = species.reshape(1, atoms)
    index = neighbour_index.reshape(slots, atoms)
    vectors = edge_vectors.reshape(3, slots, atoms)
    lists = ghost_send.reshape(3, 128)
    shape = jax.ShapeDtypeStruct

    ghosts = []
    for section, axis in enumerate(("gx", "gy", "gz")):
        chosen = call(pick_species(section), shape((8, 128), F32), (kinds, lists, *ghosts))
        ghosts += [shifted(chosen, axis, 1), shifted(chosen, axis, -1)]
    angular, hidden_one, hidden_two = call(
        geometry_kernel,
        (
            shape((atoms // 128, 16 * slots, 128), F32),
            shape((slots, 64, atoms), BF16),
            shape((slots, 64, atoms), BF16),
        ),
        (vectors, neighbour_count.reshape(1, atoms), radial_in_one, radial_in_two),
        [pltpu.VMEM((atoms // 128, BASIS * slots, 128), F32)],
    )
    second = call(
        layer_one_kernel,
        shape((atoms, 128), BF16),
        (kinds, *ghosts, index, angular, hidden_one, radial_out_one, embedding, message_one,
         self_mix, basis_mix, message_two),
        [
            pltpu.VMEM((slots, 512, atoms), F32),
            pltpu.VMEM((atoms // 128, slots, 128), F32),
            pltpu.VMEM((512, atoms), BF16),
        ],
    )
    coeffs = call(
        layer_two_kernel,
        shape((atoms, 128), BF16),
        (second, *extend(second, lists), index, angular, hidden_two, radial_out_two, decoder),
        [
            pltpu.VMEM((slots, 512, atoms), F32),
            pltpu.VMEM((2048, atoms), BF16),
            pltpu.VMEM((640, 128), F32),
        ],
    )
    table = jnp.concatenate([coeffs, *extend(coeffs, lists)], axis=0)
    column = lax.axis_size("gy")
    here = lax.axis_index("gy")
    bricks = brick_send.reshape(-1)
    bricks = jnp.concatenate([bricks, bricks])
    nearby = lax.dynamic_slice_in_dim(bricks, ((here + column - 2) % column) * 32, 160, 0)
    chosen = jnp.take(table, nearby, axis=0)
    pieces = []
    for n in range(5):
        step = 2 - n
        sent = chosen[32 * (step + 2) : 32 * (step + 3)]
        pieces.append(shifted(sent, "gy", step) if step else sent)
    density = call(
        density_kernel,
        shape((1, probes), F32),
        (jnp.stack([here, column]).astype(jnp.int32), *pieces, probe_index.reshape(slots, probes),
         probe_count.reshape(1, probes), probe_vectors.reshape(3, slots, probes)),
        [
            pltpu.VMEM((probes // 128, 16 * slots, 128), F32),
            pltpu.VMEM((probes // 128, BASIS * slots, 128), F32),
            pltpu.VMEM((256, 128), F32),
        ],
        specs=[SMEM] + [VMEM] * 8,
    )
    return density.reshape(1, 1, 1, probes)


def solution(mesh):
    domain = ("gx", "gy", "gz")
    placed = tuple(P(*domain) for _ in range(9)) + tuple(P() for _ in range(10))
    return jax.shard_map(
        shards, mesh=mesh, in_specs=placed, out_specs=P(*domain), check_vma=False
    )
```

```python
import functools
import math

import jax
import jax.numpy as jnp
from jax import lax
from jax.experimental import pallas as pl
from jax.experimental.pallas import tpu as pltpu
from jax.sharding import PartitionSpec as P

BASIS = 8
F32 = jnp.float32
BF16 = jnp.bfloat16
VMEM = pl.BlockSpec(memory_space=pltpu.VMEM)


def call(kernel, out_shape, operands, scratch=(), limit=8, flops=0, moved=1 << 20):
    many = isinstance(out_shape, (list, tuple))
    return pl.pallas_call(
        kernel,
        out_shape=out_shape,
        in_specs=[VMEM] * len(operands),
        out_specs=[VMEM] * len(out_shape) if many else VMEM,
        scratch_shapes=list(scratch),
        compiler_params=pltpu.CompilerParams(vmem_limit_bytes=limit << 20),
        cost_estimate=pl.CostEstimate(flops=flops, bytes_accessed=moved, transcendentals=0),
    )(*operands)


def dot(a, b):
    return jnp.dot(a, b, preferred_element_type=F32)


def dot_first(a, b):
    return lax.dot_general(a, b, (((0,), (0,)), ((), ())), preferred_element_type=F32)


def harmonics(vx, vy, vz, weight):
    radius = jnp.sqrt(vx * vx + vy * vy + vz * vz)
    inverse = 1.0 / radius
    x, y, z = vx * inverse, vy * inverse, vz * inverse
    xx, yy, zz = x * x, y * y, z * z
    r3, r15, r5, r105, r7 = (math.sqrt(v) for v in (3.0, 15.0, 5.0, 105.0, 7.0))
    outer, inner = math.sqrt(35.0 / 8.0), math.sqrt(21.0 / 8.0)
    rows = [
        jnp.ones_like(x),
        r3 * x,
        r3 * y,
        r3 * z,
        r15 * x * y,
        r15 * y * z,
        0.5 * r5 * (3.0 * zz - 1.0),
        r15 * x * z,
        0.5 * r15 * (xx - yy),
        outer * y * (3.0 * xx - yy),
        r105 * x * y * z,
        inner * y * (5.0 * zz - 1.0),
        0.5 * r7 * z * (5.0 * zz - 3.0),
        inner * x * (5.0 * zz - 1.0),
        0.5 * r105 * z * (xx - yy),
        outer * x * (xx - 3.0 * yy),
    ]
    return [row * weight for row in rows], radius, inverse


def radial_basis(radius, inverse, cutoff):
    u = radius * (1.0 / cutoff)
    u2 = u * u
    envelope = 1.0 + u2 * u2 * u2 * (-28.0 + u * (48.0 - 21.0 * u))
    scale = math.sqrt(2.0 / cutoff) * inverse * envelope
    angle = radius * (math.pi / cutoff)
    before, now = jnp.zeros_like(angle), jnp.sin(angle)
    twice = 2.0 * jnp.cos(angle)
    rows = []
    for _ in range(BASIS):
        rows.append(now * scale)
        before, now = now, twice * now - before
    return rows


def sections(arrays):
    return jnp.where(lax.broadcasted_iota(jnp.int32, (8, 128), 1) < 64, arrays[1], arrays[0])


def swapped(index):
    return jnp.where(index >= 256, index ^ 64, index)


def species_rows(species_ref, pieces):
    parts = [jnp.broadcast_to(species_ref[...].astype(F32), (8, 256))]
    for first in range(0, len(pieces), 2):
        parts.append(sections((pieces[first][...], pieces[first + 1][...])))
    return jnp.concatenate(parts, axis=1)


def onehot_of(chosen, rows):
    row_ids = lax.broadcasted_iota(jnp.int32, (rows, chosen.shape[1]), 0)
    return jnp.where(row_ids == chosen, 1.0, 0.0).astype(BF16)


def section_list(lists_ref, section):
    return lists_ref[:, section * 128 : (section + 1) * 128]


def pick_species(section):
    def kernel(species_ref, lists_ref, *rest):
        table = species_rows(species_ref, rest[:-1]).astype(BF16)
        chosen = swapped(section_list(lists_ref, section))
        rest[-1][...] = dot(table, onehot_of(chosen, table.shape[1]))

    return kernel


def send_rows(lists_ref, section, table, low_ref, high_ref):
    chosen = dot_first(onehot_of(section_list(lists_ref, section), table.shape[0]), table)
    high_ref[...] = chosen[:64].astype(BF16)
    low_ref[...] = chosen[64:].astype(BF16)


def pick_rows(section):
    def kernel(lists_ref, *rest):
        table = jnp.concatenate([piece[...] for piece in rest[:-2]], axis=0)
        send_rows(lists_ref, section, table, *rest[-2:])

    return kernel


def by_group(x):
    rows, lanes = x.shape
    row = lax.broadcasted_iota(jnp.int32, x.shape, 0)
    block = lax.broadcasted_iota(jnp.int32, x.shape, 1) >> 3
    step = 1
    while step < rows:
        up = pltpu.roll(pltpu.roll(x, 8 * step, axis=1), rows - step, axis=0)
        down = pltpu.roll(pltpu.roll(x, lanes - 8 * step, axis=1), step, axis=0)
        moved = jnp.where((block & step) != 0, up, down)
        x = jnp.where(((row ^ block) & step) != 0, moved, x)
        step *= 2
    return x


def store_rows(ref, rows):
    for n, row in enumerate(rows):
        size = row.shape[0]
        for tile in range(ref.shape[0]):
            ref[tile, n * size : (n + 1) * size, :] = row[:, tile * 128 : (tile + 1) * 128]


def spread(ref, row):
    parts = [ref[tile, pl.ds(row, 8, stride=0), :] for tile in range(ref.shape[0])]
    return jnp.concatenate(parts, axis=1)


def basis_rows(ref, slot, slots):
    parts = [ref[tile, pl.ds(slot, BASIS, stride=slots), :] for tile in range(ref.shape[0])]
    return jnp.concatenate(parts, axis=1)


def geometry_kernel(
    vec_ref, count_ref, index_ref, in1_ref, in2_ref, y_ref, hid1_ref, hid2_ref, where_ref, phi
):
    slots, atoms = index_ref.shape
    live = lax.broadcasted_iota(jnp.int32, (slots, atoms), 0) < count_ref[...]
    weight = by_group(jnp.where(live, 0.25, 0.0))
    vx, vy, vz = (by_group(vec_ref[n]) for n in range(3))
    rows, radius, inverse = harmonics(vx, vy, vz, weight)
    store_rows(y_ref, rows)
    store_rows(phi, radial_basis(radius, inverse, 5.0))
    where_ref[...] = by_group(index_ref[...].astype(F32)).astype(jnp.int32)
    into1 = in1_ref[...].astype(F32).T.astype(BF16)
    into2 = in2_ref[...].astype(F32).T.astype(BF16)
    for g in range(slots):
        basis = basis_rows(phi, g, slots).astype(BF16)
        for into, out in ((into1, hid1_ref), (into2, hid2_ref)):
            value = dot(into, basis)
            out[g] = (value / (1.0 + jnp.exp(-value))).astype(BF16)


def group_sums(g, groups, out_t, hid_ref, y_ref, picked):
    radial = dot(out_t, hid_ref[g])
    own = (lax.broadcasted_iota(jnp.int32, (8, 256), 1) & 7) == lax.broadcasted_iota(
        jnp.int32, (8, 256), 0
    )
    sums = []
    for degree in range(4):
        weighted = (radial[degree * 128 : (degree + 1) * 128] * picked).astype(BF16)
        angular = [
            jnp.where(own, spread(y_ref, m * groups + g), 0.0)
            for m in range(degree * degree, (degree + 1) * (degree + 1))
        ]
        total = lax.dot_general(
            jnp.concatenate(angular, axis=0).astype(BF16),
            weighted,
            (((1,), (1,)), ((), ())),
            preferred_element_type=F32,
        )
        sums += [total[8 * m : 8 * (m + 1)] for m in range(2 * degree + 1)]
    return sums


def layer_one_kernel(
    species_ref, xl, xh, yl, yh, zl, zh, where_ref, y_ref, hid_ref, out_ref, emb_ref, msg1_ref,
    self_ref, mix_ref, msg2_ref, lists_ref, next_ref, low_ref, high_ref, kinds, feats,
):
    groups, edges = where_ref.shape
    atoms = species_ref.shape[1]
    table = species_rows(species_ref, (xl, xh, yl, yh, zl, zh))
    for row in range(0, groups, 8):
        for lane in range(0, edges, 128):
            where = swapped(where_ref[row : row + 8, lane : lane + 128])
            found = jnp.zeros((8, 128), F32)
            for b in range(5):
                part = jnp.take_along_axis(table[:, b * 128 : (b + 1) * 128], where & 127, axis=1)
                found = jnp.where((where >> 7) == b, part, found)
            kinds[lane // 128, row : row + 8, :] = found
    rows_t = dot(emb_ref[...], msg1_ref[...]).astype(BF16).astype(F32).T.astype(BF16)
    out_t = out_ref[...].astype(F32).T.astype(BF16)
    kind_ids = lax.broadcasted_iota(jnp.int32, (8, 256), 0).astype(F32)

    def pair(j, carry):
        parts = []
        for g in (2 * j, 2 * j + 1):
            onehot = jnp.where(spread(kinds, g) == kind_ids, 1.0, 0.0).astype(BF16)
            sums = group_sums(g, groups, out_t, hid_ref, y_ref, dot(rows_t, onehot))
            part = [sums[0]]
            for degree in (1, 2, 3):
                part.append(sum(v * v for v in sums[degree * degree : (degree + 1) ** 2]))
            parts.append(jnp.concatenate(part, axis=1))
        first = pl.multiple_of(j * 16, 16)
        feats[pl.ds(first, 16), :] = jnp.concatenate(parts, axis=0).astype(BF16)
        return carry

    lax.fori_loop(0, groups // 2, pair, 0, unroll=2)
    own = jnp.where(table[:, :atoms] == kind_ids, 1.0, 0.0).astype(BF16)
    start = dot_first(own, emb_ref[...]).astype(BF16)
    mixed = dot(start, self_ref[...]) + dot(feats[...], mix_ref[...])
    hidden = (mixed / (1.0 + jnp.exp(-mixed))).astype(BF16)
    message = dot(hidden, msg2_ref[...]).astype(BF16)
    next_ref[...] = message
    send_rows(lists_ref, 0, message, low_ref, high_ref)


def layer_two_kernel(
    own_ref, xl, xh, yl, yh, zl, zh, where_ref, y_ref, hid_ref, out_ref, dec_ref, lists_ref,
    coeff_ref, low_ref, high_ref, feats,
):
    groups, edges = where_ref.shape
    pieces = [piece[...].astype(F32) for piece in (own_ref, xl, xh, yl, yh, zl, zh)]
    table = jnp.concatenate(pieces + [jnp.zeros((128, 128), F32)], axis=0)
    rows_t = jnp.concatenate([table[256 * n : 256 * (n + 1)].T for n in range(3)], axis=0)
    rows_t = rows_t.astype(BF16)
    out_t = out_ref[...].astype(F32).T.astype(BF16)

    def pair(j, carry):
        parts = []
        for g in (2 * j, 2 * j + 1):
            where = where_ref[pl.ds(g, 1), :]
            found = dot(rows_t, onehot_of(where & 255, 256))
            picked = jnp.where(where < 256, found[:128], found[128:256])
            picked = jnp.where(where < 512, picked, found[256:])
            sums = group_sums(g, groups, out_t, hid_ref, y_ref, picked)
            parts.append(jnp.concatenate(sums, axis=1))
        first = pl.multiple_of(j * 16, 16)
        feats[pl.ds(first, 16), :] = jnp.concatenate(parts, axis=0).astype(BF16)
        return carry

    lax.fori_loop(0, groups // 2, pair, 0, unroll=2)
    column = lax.broadcasted_iota(jnp.int32, (8, 128), 1)
    repeat = (column & 7) == lax.broadcasted_iota(jnp.int32, (8, 128), 0)
    repeat = jnp.where(repeat, 1.0, 0.0).astype(BF16)
    group = lax.broadcasted_iota(jnp.int32, (128, 128), 1) >> 3
    blocks = []
    for degree in range(4):
        wide = dot_first(dec_ref[degree], repeat)
        for m in range(degree * degree, (degree + 1) * (degree + 1)):
            blocks.append(jnp.where(group == m, wide, 0.0).astype(BF16))
    coeffs = dot(feats[...], jnp.concatenate(blocks, axis=0)).astype(BF16)
    coeff_ref[...] = coeffs
    send_rows(lists_ref, 0, coeffs, low_ref, high_ref)


def brick_kernel(list_ref, *rest):
    table = jnp.concatenate([piece[...] for piece in rest[:7]], axis=0)
    chosen = dot_first(onehot_of(list_ref[...], table.shape[0]), table).astype(BF16)
    for n in range(5):
        rest[7 + n][...] = chosen[32 * n : 32 * (n + 1)]


def probe_kernel(list_ref, count_ref, vec_ref, y_ref, phi_ref):
    slots, probes = vec_ref.shape[1:]
    live = lax.broadcasted_iota(jnp.int32, (slots, probes), 0) < count_ref[...]
    weight = jnp.where(live, 0.125, 0.0)
    rows, radius, inverse = harmonics(vec_ref[0], vec_ref[1], vec_ref[2], weight)
    store_rows(y_ref, rows)
    store_rows(phi_ref, radial_basis(radius, inverse, 4.0))


def density_kernel(column, p0, p1, p2, p3, p4, index_ref, y, phi, out_ref):
    slots, probes = index_ref.shape
    here = lax.axis_index("gy")
    pieces = [piece[...].astype(F32) for piece in (p0, p1, p2, p3, p4)]
    table = jnp.concatenate(pieces + [jnp.zeros((96, 128), F32)], axis=0)
    rows_t = table.T[:, :160].astype(BF16)

    def slot(k, total):
        index = index_ref[pl.ds(k, 1), :]
        source = (index >> 5) - here + 2
        source = jnp.where(source < 0, source + column, source)
        source = jnp.where(source >= column, source - column, source)
        picked = dot(rows_t, onehot_of(source * 32 + (index & 31), 160))
        part = jnp.zeros((8, probes), F32)
        for m in range(16):
            part = part + spread(y, m * slots + k) * picked[m * 8 : (m + 1) * 8]
        return total + part * basis_rows(phi, k, slots)

    total = lax.fori_loop(0, slots, slot, jnp.zeros((8, probes), F32), unroll=2)
    out_ref[...] = jnp.sum(total, axis=0, keepdims=True)


def shifted(block, axis, step):
    size = lax.axis_size(axis)
    return lax.ppermute(block, axis, [(i, (i + step) % size) for i in range(size)])


def extend(rows, low, high, lists):
    half = jax.ShapeDtypeStruct((64, 128), BF16)
    pieces = []
    for section, axis in enumerate(("gx", "gy", "gz")):
        if section:
            low, high = call(pick_rows(section), (half, half), (lists, rows, *pieces))
        pieces += [shifted(low, axis, 1), shifted(high, axis, -1)]
    return pieces


def shards(
    species, neighbour_index, neighbour_count, edge_vectors, ghost_send, brick_send, probe_index,
    probe_count, probe_vectors, embedding, message_one, radial_in_one, radial_out_one, self_mix,
    basis_mix, message_two, radial_in_two, radial_out_two, decoder,
):
    slots, atoms = neighbour_index.shape[3:]
    probes = probe_index.shape[-1]
    kinds = species.reshape(1, atoms)
    lists = ghost_send.reshape(1, 384)
    shape = jax.ShapeDtypeStruct
    half = shape((64, 128), BF16)
    column = lax.axis_size("gy")
    here = lax.axis_index("gy")

    ghosts = []
    for section, axis in enumerate(("gx", "gy", "gz")):
        chosen = call(pick_species(section), shape((8, 128), F32), (kinds, lists, *ghosts))
        ghosts += [shifted(chosen, axis, 1), shifted(chosen, axis, -1)]
    angular, hidden_one, hidden_two, where = call(
        geometry_kernel,
        (
            shape((2, 16 * slots, 128), F32),
            shape((slots, 64, atoms), BF16),
            shape((slots, 64, atoms), BF16),
            shape((slots, atoms), jnp.int32),
        ),
        (
            edge_vectors.reshape(3, slots, atoms),
            neighbour_count.reshape(1, atoms),
            neighbour_index.reshape(slots, atoms),
            radial_in_one,
            radial_in_two,
        ),
        [pltpu.VMEM((2, BASIS * slots, 128), F32)],
    )
    probe_y, probe_phi = call(
        probe_kernel,
        (shape((probes // 128, 16 * slots, 128), F32), shape((probes // 128, 256, 128), F32)),
        (lists, probe_count.reshape(1, probes), probe_vectors.reshape(3, slots, probes)),
    )
    bricks = brick_send.reshape(1, -1)
    bricks = jnp.concatenate([bricks, bricks], axis=1)
    nearby = lax.dynamic_slice_in_dim(bricks, ((here + column - 2) % column) * 32, 160, 1)
    second = call(
        layer_one_kernel,
        (shape((atoms, 128), BF16), half, half),
        (kinds, *ghosts, where, angular, hidden_one, radial_out_one, embedding, message_one,
         self_mix, basis_mix, message_two, lists),
        [pltpu.VMEM((2, slots, 128), F32), pltpu.VMEM((atoms, 512), BF16)],
        limit=16,
    )
    coeffs = call(
        layer_two_kernel,
        (shape((atoms, 128), BF16), half, half),
        (second[0], *extend(*second, lists), where, angular, hidden_two, radial_out_two,
         decoder.transpose(0, 2, 1), lists),
        [pltpu.VMEM((atoms, 2048), BF16)],
        limit=16,
    )
    sent = call(
        brick_kernel, [shape((32, 128), BF16)] * 5, (nearby, coeffs[0], *extend(*coeffs, lists))
    )
    pieces = []
    for n in range(5):
        step = 2 - n
        pieces.append(shifted(sent[step + 2], "gy", step) if step else sent[2])
    density = call(
        functools.partial(density_kernel, column),
        shape((1, probes), F32),
        (*pieces, probe_index.reshape(slots, probes), probe_y, probe_phi),
    )
    return density.reshape(1, 1, 1, probes)


def solution(mesh):
    domain = ("gx", "gy", "gz")
    placed = tuple(P(*domain) for _ in range(9)) + tuple(P() for _ in range(10))
    return jax.shard_map(
        shards, mesh=mesh, in_specs=placed, out_specs=P(*domain), check_vma=False
    )
```

```python
import functools
import math

import jax
import jax.numpy as jnp
from jax import lax
from jax.experimental import pallas as pl
from jax.experimental.pallas import tpu as pltpu
from jax.sharding import PartitionSpec as P

BASIS = 8
F32 = jnp.float32
BF16 = jnp.bfloat16
VMEM = pl.BlockSpec(memory_space=pltpu.VMEM)
ANY = pl.BlockSpec(memory_space=pl.ANY)


def call(kernel, out_shape, operands, scratch=(), limit=8, after=()):
    count = len(operands)

    def body(*refs):
        kernel(*refs[:count], *refs[count + len(after) :])

    return pl.pallas_call(
        body,
        out_shape=out_shape,
        in_specs=[VMEM] * count + [ANY] * len(after),
        out_specs=jax.tree.map(lambda _: VMEM, out_shape),
        scratch_shapes=list(scratch),
        compiler_params=pltpu.CompilerParams(vmem_limit_bytes=limit and limit << 20),
        cost_estimate=pl.CostEstimate(flops=0, bytes_accessed=1 << 20, transcendentals=0),
    )(*operands, *after)


def dot(a, b):
    return jnp.dot(a, b, preferred_element_type=F32)


def dot_first(a, b):
    return lax.dot_general(a, b, (((0,), (0,)), ((), ())), preferred_element_type=F32)


def harmonics(vx, vy, vz, weight):
    radius = jnp.sqrt(vx * vx + vy * vy + vz * vz)
    inverse = 1.0 / radius
    x, y, z = vx * inverse, vy * inverse, vz * inverse
    xx, yy, zz = x * x, y * y, z * z
    r3, r15, r5, r105, r7 = (math.sqrt(v) for v in (3.0, 15.0, 5.0, 105.0, 7.0))
    outer, inner = math.sqrt(35.0 / 8.0), math.sqrt(21.0 / 8.0)
    rows = [
        jnp.ones_like(x),
        r3 * x,
        r3 * y,
        r3 * z,
        r15 * x * y,
        r15 * y * z,
        0.5 * r5 * (3.0 * zz - 1.0),
        r15 * x * z,
        0.5 * r15 * (xx - yy),
        outer * y * (3.0 * xx - yy),
        r105 * x * y * z,
        inner * y * (5.0 * zz - 1.0),
        0.5 * r7 * z * (5.0 * zz - 3.0),
        inner * x * (5.0 * zz - 1.0),
        0.5 * r105 * z * (xx - yy),
        outer * x * (xx - 3.0 * yy),
    ]
    return [row * weight for row in rows], radius, inverse


def radial_basis(radius, inverse, cutoff):
    u = radius * (1.0 / cutoff)
    u2 = u * u
    envelope = 1.0 + u2 * u2 * u2 * (-28.0 + u * (48.0 - 21.0 * u))
    scale = math.sqrt(2.0 / cutoff) * inverse * envelope
    angle = radius * (math.pi / cutoff)
    before, now = jnp.zeros_like(angle), jnp.sin(angle)
    twice = 2.0 * jnp.cos(angle)
    rows = []
    for _ in range(BASIS):
        rows.append(now * scale)
        before, now = now, twice * now - before
    return rows


def sections(arrays):
    return jnp.where(lax.broadcasted_iota(jnp.int32, (8, 128), 1) < 64, arrays[1], arrays[0])


def swapped(index):
    return jnp.where(index >= 256, index ^ 64, index)


def species_rows(species_ref, pieces):
    parts = [jnp.broadcast_to(species_ref[...].astype(F32), (8, 256))]
    for first in range(0, len(pieces), 2):
        parts.append(sections((pieces[first][...], pieces[first + 1][...])))
    return jnp.concatenate(parts, axis=1)


def onehot_of(chosen, rows):
    row_ids = lax.broadcasted_iota(jnp.int32, (rows, chosen.shape[1]), 0)
    return jnp.where(row_ids == chosen, 1.0, 0.0).astype(BF16)


def section_list(lists_ref, section):
    return lists_ref[:, section * 128 : (section + 1) * 128]


def pick_species(section):
    def kernel(species_ref, lists_ref, *rest):
        pieces, out_ref = rest[: 2 * section], rest[2 * section]
        table = species_rows(species_ref, pieces).astype(BF16)
        chosen = swapped(section_list(lists_ref, section))
        out_ref[...] = dot(table, onehot_of(chosen, table.shape[1]))

    return kernel


def first_kernel(species_ref, lists_ref, out_ref, species_copy, lists_copy):
    pick_species(0)(species_ref, lists_ref, out_ref)
    species_copy[...] = species_ref[...]
    lists_copy[...] = lists_ref[...]


def send_rows(lists_ref, section, table, low_ref, high_ref):
    chosen = dot_first(onehot_of(section_list(lists_ref, section), table.shape[0]), table)
    high_ref[...] = chosen[:64].astype(BF16)
    low_ref[...] = chosen[64:].astype(BF16)


def pick_rows(section):
    def kernel(lists_ref, *rest):
        table = jnp.concatenate([piece[...] for piece in rest[:-2]], axis=0)
        send_rows(lists_ref, section, table, *rest[-2:])

    return kernel


def by_group(x):
    rows, lanes = x.shape
    row = lax.broadcasted_iota(jnp.int32, x.shape, 0)
    block = lax.broadcasted_iota(jnp.int32, x.shape, 1) >> 3
    step = 1
    while step < rows:
        up = pltpu.roll(pltpu.roll(x, 8 * step, axis=1), rows - step, axis=0)
        down = pltpu.roll(pltpu.roll(x, lanes - 8 * step, axis=1), step, axis=0)
        moved = jnp.where((block & step) != 0, up, down)
        x = jnp.where(((row ^ block) & step) != 0, moved, x)
        step *= 2
    return x


def store_rows(ref, rows):
    for n, row in enumerate(rows):
        size = row.shape[0]
        for tile in range(ref.shape[0]):
            ref[tile, n * size : (n + 1) * size, :] = row[:, tile * 128 : (tile + 1) * 128]


def spread(ref, row):
    parts = [ref[tile, pl.ds(row, 8, stride=0), :] for tile in range(ref.shape[0])]
    return jnp.concatenate(parts, axis=1)


def basis_rows(ref, slot, slots):
    parts = [ref[tile, pl.ds(slot, BASIS, stride=slots), :] for tile in range(ref.shape[0])]
    return jnp.concatenate(parts, axis=1)


def transposed(ref):
    return ref[...].astype(F32).T.astype(BF16)


def hidden_rows(phi_ref, in_ref, hid_ref):
    groups = hid_ref.shape[0]
    into = transposed(in_ref)
    for g in range(groups):
        value = dot(into, basis_rows(phi_ref, g, groups).astype(BF16))
        hid_ref[g] = (value / (1.0 + jnp.exp(-value))).astype(BF16)


def radial_rows(first, hid_ref, out_ref, radial_ref):
    def step(g, carry):
        radial_ref[g] = dot_first(hid_ref[first + g], out_ref[...])
        return carry

    lax.fori_loop(0, radial_ref.shape[0], step, 0, unroll=2)


def geometry_kernel(
    vec_ref, count_ref, index_ref, y_ref, phi_ref, where_ref
):
    slots, atoms = index_ref.shape
    live = lax.broadcasted_iota(jnp.int32, (slots, atoms), 0) < count_ref[...]
    weight = by_group(jnp.where(live, 0.25, 0.0))
    vx, vy, vz = (by_group(vec_ref[n]) for n in range(3))
    rows, radius, inverse = harmonics(vx, vy, vz, weight)
    store_rows(y_ref, rows)
    store_rows(phi_ref, radial_basis(radius, inverse, 5.0))
    where_ref[...] = by_group(index_ref[...].astype(F32)).astype(jnp.int32)


def first_radial_kernel(
    phi_ref, in_ref, out_ref, emb_ref, msg_ref, hid_ref, rows_ref, radial_ref
):
    rows_ref[...] = dot(emb_ref[...], msg_ref[...]).astype(BF16)
    hidden_rows(phi_ref, in_ref, hid_ref)
    radial_rows(0, hid_ref, out_ref, radial_ref)


def radial_kernel(first):
    def kernel(hid_ref, out_ref, radial_ref):
        radial_rows(first, hid_ref, out_ref, radial_ref)

    return kernel


def second_radial_kernel(phi_ref, in_ref, out_ref, hid_ref, radial_ref):
    hidden_rows(phi_ref, in_ref, hid_ref)
    radial_rows(0, hid_ref, out_ref, radial_ref)


def last_radial_kernel(first):
    def kernel(hid_ref, out_ref, dec_ref, radial_ref, blocks_ref):
        radial_rows(first, hid_ref, out_ref, radial_ref)
        column = lax.broadcasted_iota(jnp.int32, (8, 128), 1)
        repeat = (column & 7) == lax.broadcasted_iota(jnp.int32, (8, 128), 0)
        repeat = jnp.where(repeat, 1.0, 0.0).astype(BF16)
        group = lax.broadcasted_iota(jnp.int32, (128, 128), 1) >> 3
        for degree in range(4):
            wide = dot_first(dec_ref[degree], repeat)
            for m in range(degree * degree, (degree + 1) * (degree + 1)):
                block = jnp.where(group == m, wide, 0.0).astype(BF16)
                blocks_ref[m * 128 : (m + 1) * 128, :] = block

    return kernel


def group_sums(g, groups, radial, y_ref, picked):
    own = (lax.broadcasted_iota(jnp.int32, (8, 256), 1) & 7) == lax.broadcasted_iota(
        jnp.int32, (8, 256), 0
    )
    twice = jnp.concatenate([picked, picked], axis=1)
    sums = []
    for degrees, first, last in (((0, 1), 0, 4), ((2, 3), 4, 16)):
        lane = degrees[0] * 128
        weighted = (radial[:, lane : lane + 256] * twice).astype(BF16)
        angular = [jnp.where(own, spread(y_ref, m * groups + g), 0.0) for m in range(first, last)]
        total = dot(jnp.concatenate(angular, axis=0).astype(BF16), weighted)
        for m in range(first, last):
            side = 0 if m < (degrees[0] + 1) ** 2 else 128
            sums.append(total[8 * (m - first) : 8 * (m - first + 1), side : side + 128])
    return sums


def each_pair(radials, pair):
    first = 0
    for radial in radials:

        def step(j, carry, first=first, radial=radial):
            groups = [(first + 2 * j + n, radial.at[2 * j + n]) for n in range(2)]
            pair(pl.multiple_of((first + 2 * j) * 8, 16), groups)
            return carry

        lax.fori_loop(0, radial.shape[0] // 2, step, 0, unroll=4)
        first += radial.shape[0]


def layer_one_kernel(
    species_ref, xl, xh, yl, yh, zl, zh, where_ref, y_ref, radial_a, radial_b, rows_ref, emb_ref,
    self_ref, mix_ref, msg2_ref, lists_ref, next_ref, low_ref, high_ref, onehot, feats,
):
    groups, edges = where_ref.shape
    atoms = species_ref.shape[1]
    table = species_rows(species_ref, (xl, xh, yl, yh, zl, zh))
    blocks = []
    for lane in range(0, edges, 128):
        column = []
        for row in range(0, groups, 8):
            where = swapped(where_ref[row : row + 8, lane : lane + 128])
            found = jnp.zeros((8, 128), F32)
            for b in range(5):
                part = jnp.take_along_axis(table[:, b * 128 : (b + 1) * 128], where & 127, axis=1)
                found = jnp.where((where >> 7) == b, part, found)
            column.append(found)
        blocks.append(jnp.concatenate(column, axis=0))
    kinds = jnp.concatenate(blocks, axis=1).T.astype(BF16)
    lane_group = lax.broadcasted_iota(jnp.int32, (groups, 8 * groups), 1) >> 3
    widen = lane_group == lax.broadcasted_iota(jnp.int32, (groups, 8 * groups), 0)
    kinds = dot(kinds, jnp.where(widen, 1.0, 0.0).astype(BF16))
    kind_of_lane = lax.broadcasted_iota(jnp.int32, kinds.shape, 1) & 7
    onehot[...] = jnp.where(kinds == kind_of_lane.astype(F32), 1.0, 0.0).astype(BF16)
    tall = jnp.concatenate([rows_ref[...].astype(F32)] * groups, axis=0)
    row_group = lax.broadcasted_iota(jnp.int32, tall.shape, 0) >> 3

    def pair(row, members):
        parts = []
        own_rows = [jnp.where(row_group == g, tall, 0.0) for g, _ in members]
        found = dot(onehot[...], jnp.concatenate(own_rows, axis=1).astype(BF16))
        for n, (g, radial) in enumerate(members):
            sums = group_sums(g, groups, radial, y_ref, found[:, 128 * n : 128 * (n + 1)])
            part = [sums[0]]
            for degree in (1, 2, 3):
                part.append(sum(v * v for v in sums[degree * degree : (degree + 1) ** 2]))
            parts.append(jnp.concatenate(part, axis=1))
        feats[pl.ds(row, 16), :] = jnp.concatenate(parts, axis=0).astype(BF16)

    each_pair((radial_a, radial_b), pair)
    kind_ids = lax.broadcasted_iota(jnp.int32, (8, atoms), 0).astype(F32)
    own = jnp.where(table[:, :atoms] == kind_ids, 1.0, 0.0).astype(BF16)
    start = dot_first(own, emb_ref[...]).astype(BF16)
    mixed = dot(start, self_ref[...]) + dot(feats[...], mix_ref[...])
    hidden = (mixed / (1.0 + jnp.exp(-mixed))).astype(BF16)
    message = dot(hidden, msg2_ref[...]).astype(BF16)
    next_ref[...] = message
    send_rows(lists_ref, 0, message, low_ref, high_ref)


def layer_two_kernel(
    own_ref, xl, xh, yl, yh, zl, zh, where_ref, y_ref, radial_a, radial_b, radial_c, blocks_ref,
    lists_ref, coeff_ref, low_ref, high_ref, feats, wide, index,
):
    groups, edges = where_ref.shape
    pieces = [piece[...].astype(F32) for piece in (own_ref, xl, xh, yl, yh, zl, zh)]
    table = jnp.concatenate(pieces + [jnp.zeros((128, 128), F32)], axis=0)
    table = jnp.concatenate([table[256 * n : 256 * (n + 1)] for n in range(3)], axis=1)
    wide[...] = table[:, :384].astype(BF16)
    halves = (where_ref[...] & 255, where_ref[...] >> 8)
    index[...] = jnp.concatenate([half.astype(F32).T for half in halves], axis=1).astype(BF16)
    source = lax.broadcasted_iota(jnp.int32, (2 * groups, 512), 0)
    target = lax.broadcasted_iota(jnp.int32, (2 * groups, 512), 1) >> 7
    low_ids = lax.broadcasted_iota(jnp.int32, (edges, 128), 1).astype(F32)

    def pair(row, members):
        parts, onehots = [], []
        first = members[0][0]
        picks = source == first + (target & 1) + jnp.where(target < 2, 0, groups)
        spread_index = dot(index[...], jnp.where(picks, 1.0, 0.0).astype(BF16))
        for n in range(2):
            low = spread_index[:, 128 * n : 128 * (n + 1)]
            sides = [jnp.where(low == low_ids + 128.0 * side, 1.0, 0.0) for side in range(2)]
            onehots.append(jnp.concatenate(sides, axis=1))
        found = dot(jnp.concatenate(onehots, axis=0).astype(BF16), wide[...])
        for n, (g, radial) in enumerate(members):
            high = spread_index[:, 256 + 128 * n : 384 + 128 * n]
            mine = found[edges * n : edges * (n + 1)]
            picked = jnp.where(high < 0.5, mine[:, :128], mine[:, 128:256])
            picked = jnp.where(high < 1.5, picked, mine[:, 256:])
            sums = group_sums(g, groups, radial, y_ref, picked)
            parts.append(jnp.concatenate(sums, axis=1))
        feats[pl.ds(row, 16), :] = jnp.concatenate(parts, axis=0).astype(BF16)

    each_pair((radial_a, radial_b, radial_c), pair)
    coeffs = dot(feats[...], blocks_ref[...]).astype(BF16)
    coeff_ref[...] = coeffs
    send_rows(lists_ref, 0, coeffs, low_ref, high_ref)


SWAPS = ((2, 1), (1, 1), (2, 0), (1, 0))


def partner_slot(distance, first):
    ahead = (lax.axis_index("gy") // distance) % 2 == first
    return jnp.where(ahead, 2 + distance, 2 - distance)


def brick_kernel(list_ref, *rest):
    pieces, outs, chosen = rest[:7], rest[7:12], rest[12]
    table = jnp.concatenate([piece[...] for piece in pieces], axis=0)
    chosen[...] = dot_first(onehot_of(list_ref[...], table.shape[0]), table)
    for swap, out in zip(SWAPS, outs):
        first = pl.multiple_of(partner_slot(*swap) * 32, 32)
        out[...] = chosen[pl.ds(first, 32), :].astype(BF16)
    outs[4][...] = chosen[64:96].astype(BF16)


def probe_kernel(
    column, list_ref, count_ref, vec_ref, index_ref, y_ref, phi_ref, where_ref, nearby_ref
):
    slots, probes = index_ref.shape
    live = lax.broadcasted_iota(jnp.int32, (slots, probes), 0) < count_ref[...]
    weight = jnp.where(live, 0.125, 0.0)
    rows, radius, inverse = harmonics(vec_ref[0], vec_ref[1], vec_ref[2], weight)
    store_rows(y_ref, rows)
    store_rows(phi_ref, radial_basis(radius, inverse, 4.0))
    here = lax.axis_index("gy")
    index = index_ref[...]
    source = (index >> 5) - here + 2
    source = jnp.where(source < 0, source + column, source)
    source = jnp.where(source >= column, source - column, source)
    where_ref[...] = source * 32 + (index & 31)
    targets = list_ref.shape[1]
    start = (2 - here) * (targets // column)
    start = jnp.where(start < 0, start + targets, start)
    turned = pltpu.roll(jnp.broadcast_to(list_ref[...], (8, targets)), start, axis=1)
    nearby_ref[...] = turned[:1, :256]


def density_kernel(p0, p1, p2, p3, p4, where_ref, y, phi, out_ref, table):
    slots, probes = where_ref.shape
    table[160:, :] = jnp.zeros((96, 128), F32)
    table[64:96, :] = p4[...].astype(F32)
    for swap, piece in zip(SWAPS, (p0, p1, p2, p3)):
        first = pl.multiple_of(partner_slot(*swap) * 32, 32)
        table[pl.ds(first, 32), :] = piece[...].astype(F32)
    rows_t = table[...].T[:, :160].astype(BF16)

    def slot(k, total):
        picked = dot(rows_t, onehot_of(where_ref[pl.ds(k, 1), :], 160))
        part = jnp.zeros((8, probes), F32)
        for m in range(16):
            part = part + spread(y, m * slots + k) * picked[m * 8 : (m + 1) * 8]
        return total + part * basis_rows(phi, k, slots)

    total = lax.fori_loop(0, slots, slot, jnp.zeros((8, probes), F32), unroll=4)
    out_ref[...] = jnp.sum(total, axis=0, keepdims=True)


def shifted(block, axis, step):
    size = lax.axis_size(axis)
    return lax.ppermute(block, axis, [(i, (i + step) % size) for i in range(size)])


def swapped_with(block, distance, first):
    size = lax.axis_size("gy")
    pairs = []
    for low in range(size):
        if (low // distance) % 2 == first:
            high = (low + distance) % size
            pairs += [(low, high), (high, low)]
    return lax.ppermute(block, "gy", sorted(pairs))


def extend(rows, low, high, lists, fillers):
    half = jax.ShapeDtypeStruct((64, 128), BF16)
    pieces, made, begin = [], [], rows
    for section, axis in enumerate(("gx", "gy", "gz")):
        if section:
            done = made[-1][-1:] if made[-1] else ()
            low, high = call(
                pick_rows(section), (half, half), (lists, rows, *pieces), after=done
            )
            begin = low
        pieces += [shifted(low, axis, 1), shifted(high, axis, -1)]
        made.append(fillers[section](made, begin) if fillers[section] else ())
    return pieces, made


def shards(
    species, neighbour_index, neighbour_count, edge_vectors, ghost_send, brick_send, probe_index,
    probe_count, probe_vectors, embedding, message_one, radial_in_one, radial_out_one, self_mix,
    basis_mix, message_two, radial_in_two, radial_out_two, decoder,
):
    slots, atoms = neighbour_index.shape[3:]
    probes = probe_index.shape[-1]
    kinds = species.reshape(1, atoms)
    lists = ghost_send.reshape(1, 384)
    shape = jax.ShapeDtypeStruct
    half = shape((64, 128), BF16)
    column = lax.axis_size("gy")

    def both(block, axis):
        return [shifted(block, axis, 1), shifted(block, axis, -1)]

    row = shape((8, 128), F32)
    hidden = shape((slots, 64, atoms), BF16)

    def radial(count):
        return shape((count, atoms, 512), F32)

    chosen, kinds, lists = call(
        first_kernel,
        (row, shape(kinds.shape, jnp.int32), shape(lists.shape, jnp.int32)),
        (kinds, lists),
    )
    ghosts = both(chosen, "gx")
    angular, phi, where = call(
        geometry_kernel,
        (
            shape((2, 16 * slots, 128), F32),
            shape((2, BASIS * slots, 128), F32),
            shape((slots, atoms), jnp.int32),
        ),
        (
            edge_vectors.reshape(3, slots, atoms),
            neighbour_count.reshape(1, atoms),
            neighbour_index.reshape(slots, atoms),
        ),
        after=(chosen,),
    )
    chosen = call(pick_species(1), row, (kinds, lists, *ghosts), after=(where,))
    ghosts += both(chosen, "gy")
    hidden_one, rows, radial_a = call(
        first_radial_kernel,
        (hidden, shape((8, 128), BF16), radial(16)),
        (phi, radial_in_one, radial_out_one, embedding, message_one),
        limit=20,
        after=(chosen,),
    )
    chosen = call(pick_species(2), row, (kinds, lists, *ghosts), after=(radial_a,))
    ghosts += both(chosen, "gz")
    radial_b = call(radial_kernel(16), radial(16), (hidden_one, radial_out_one), limit=20, after=(chosen,))
    second = call(
        layer_one_kernel,
        (shape((atoms, 128), BF16), half, half),
        (kinds, *ghosts, where, angular, radial_a, radial_b, rows, embedding, self_mix,
         basis_mix, message_two, lists),
        [pltpu.VMEM((atoms, 256), BF16), pltpu.VMEM((atoms, 512), BF16)],
        limit=16,
    )
    pieces, made = extend(
        *second,
        lists,
        (
            lambda made, begin: call(
                second_radial_kernel,
                (hidden, radial(8)),
                (phi, radial_in_two, radial_out_two),
                limit=20,
                after=(begin,),
            ),
            lambda made, begin: (
                call(
                    radial_kernel(8),
                    radial(16),
                    (made[0][0], radial_out_two),
                    limit=20,
                    after=(begin,),
                ),
            ),
            lambda made, begin: call(
                last_radial_kernel(24),
                (radial(8), shape((2048, 128), BF16)),
                (made[0][0], radial_out_two, decoder.transpose(0, 2, 1)),
                limit=20,
                after=(begin,),
            ),
        ),
    )
    coeffs = call(
        layer_two_kernel,
        (shape((atoms, 128), BF16), half, half),
        (second[0], *pieces, where, angular, made[0][1], made[1][0], *made[2], lists),
        [
            pltpu.VMEM((atoms, 2048), BF16),
            pltpu.VMEM((256, 384), BF16),
            pltpu.VMEM((atoms, 2 * slots), BF16),
        ],
        limit=16,
    )
    pieces, made = extend(
        *coeffs,
        lists,
        (
            lambda made, begin: call(
                functools.partial(probe_kernel, column),
                (
                    shape((probes // 128, 16 * slots, 128), F32),
                    shape((probes // 128, BASIS * slots, 128), F32),
                    shape((slots, probes), jnp.int32),
                    shape((1, 256), jnp.int32),
                ),
                (
                    brick_send.reshape(1, -1),
                    probe_count.reshape(1, probes),
                    probe_vectors.reshape(3, slots, probes),
                    probe_index.reshape(slots, probes),
                ),
                after=(begin,),
            ),
            None,
            None,
        ),
    )
    probe_y, probe_phi, probe_where, nearby = made[0]
    sent = call(
        brick_kernel,
        [shape((32, 128), BF16)] * 5,
        (nearby, coeffs[0], *pieces),
        [pltpu.VMEM((256, 128), F32)],
    )
    pieces = [swapped_with(sent[n], *SWAPS[n]) for n in (3, 2, 1, 0)][::-1] + [sent[4]]
    density = call(
        density_kernel,
        shape((1, probes), F32),
        (*pieces, probe_where, probe_y, probe_phi),
        [pltpu.VMEM((256, 128), F32)],
    )
    return density.reshape(1, 1, 1, probes)


def solution(mesh):
    domain = ("gx", "gy", "gz")
    placed = tuple(P(*domain) for _ in range(9)) + tuple(P() for _ in range(10))
    return jax.shard_map(
        shards, mesh=mesh, in_specs=placed, out_specs=P(*domain), check_vma=False
    )
```

```python
import functools
import math

import jax
import jax.numpy as jnp
from jax import lax
from jax.experimental import pallas as pl
from jax.experimental.pallas import tpu as pltpu
from jax.sharding import PartitionSpec as P

BASIS = 8
F32 = jnp.float32
BF16 = jnp.bfloat16
VMEM = pl.BlockSpec(memory_space=pltpu.VMEM)
HBM = pl.BlockSpec(memory_space=pltpu.HBM)
ANY = pl.BlockSpec(memory_space=pl.ANY)


def call(kernel, out_shape, operands, scratch=(), limit=8, staged=(), after=()):
    first, last = len(staged), len(staged) + len(operands)

    def body(*refs):
        if not staged:
            return kernel(*refs[:last], *refs[last + len(after) :])
        buffers, arrived = refs[-1 - first : -1], refs[-1]
        copies = [
            pltpu.make_async_copy(source, target, arrived.at[n])
            for n, (source, target) in enumerate(zip(refs, buffers))
        ]
        for copy in copies:
            copy.start()
        for copy in copies:
            copy.wait()
        kernel(*buffers, *refs[first:last], *refs[last + len(after) : -1 - first])

    room = [pltpu.VMEM(x.shape, x.dtype) for x in staged]
    if staged:
        room.append(pltpu.SemaphoreType.DMA((first,)))
    held = [pltpu.with_memory_space_constraint(x, pltpu.HBM) for x in staged]
    return pl.pallas_call(
        body,
        out_shape=out_shape,
        in_specs=[HBM] * first + [VMEM] * len(operands) + [ANY] * len(after),
        out_specs=jax.tree.map(lambda _: VMEM, out_shape),
        scratch_shapes=[*scratch, *room],
        compiler_params=pltpu.CompilerParams(vmem_limit_bytes=limit << 20),
        cost_estimate=pl.CostEstimate(flops=0, bytes_accessed=1 << 20, transcendentals=0),
    )(*held, *operands, *after)


def dot(a, b):
    return jnp.dot(a, b, preferred_element_type=F32)


def dot_first(a, b):
    return lax.dot_general(a, b, (((0,), (0,)), ((), ())), preferred_element_type=F32)


def harmonics(vx, vy, vz, weight):
    radius = jnp.sqrt(vx * vx + vy * vy + vz * vz)
    inverse = 1.0 / radius
    x, y, z = vx * inverse, vy * inverse, vz * inverse
    xx, yy, zz = x * x, y * y, z * z
    r3, r15, r5, r105, r7 = (math.sqrt(v) for v in (3.0, 15.0, 5.0, 105.0, 7.0))
    outer, inner = math.sqrt(35.0 / 8.0), math.sqrt(21.0 / 8.0)
    rows = [
        jnp.ones_like(x),
        r3 * x,
        r3 * y,
        r3 * z,
        r15 * x * y,
        r15 * y * z,
        0.5 * r5 * (3.0 * zz - 1.0),
        r15 * x * z,
        0.5 * r15 * (xx - yy),
        outer * y * (3.0 * xx - yy),
        r105 * x * y * z,
        inner * y * (5.0 * zz - 1.0),
        0.5 * r7 * z * (5.0 * zz - 3.0),
        inner * x * (5.0 * zz - 1.0),
        0.5 * r105 * z * (xx - yy),
        outer * x * (xx - 3.0 * yy),
    ]
    return [row * weight for row in rows], radius, inverse


def radial_basis(radius, inverse, cutoff):
    u = radius * (1.0 / cutoff)
    u2 = u * u
    envelope = 1.0 + u2 * u2 * u2 * (-28.0 + u * (48.0 - 21.0 * u))
    scale = math.sqrt(2.0 / cutoff) * inverse * envelope
    angle = radius * (math.pi / cutoff)
    before, now = jnp.zeros_like(angle), jnp.sin(angle)
    twice = 2.0 * jnp.cos(angle)
    rows = []
    for _ in range(BASIS):
        rows.append(now * scale)
        before, now = now, twice * now - before
    return rows


def sections(arrays):
    return jnp.where(lax.broadcasted_iota(jnp.int32, (8, 128), 1) < 64, arrays[1], arrays[0])


def swapped(index):
    return jnp.where(index >= 256, index ^ 64, index)


def species_rows(species_ref, pieces):
    parts = [jnp.broadcast_to(species_ref[...].astype(F32), (8, 256))]
    for first in range(0, len(pieces), 2):
        parts.append(sections((pieces[first][...], pieces[first + 1][...])))
    return jnp.concatenate(parts, axis=1)


def onehot_of(chosen, rows):
    row_ids = lax.broadcasted_iota(jnp.int32, (rows, chosen.shape[1]), 0)
    return jnp.where(row_ids == chosen, 1.0, 0.0).astype(BF16)


def section_list(lists_ref, section):
    return lists_ref[:, section * 128 : (section + 1) * 128]


def pick_species(section):
    def kernel(species_ref, lists_ref, *rest):
        pieces, out_ref = rest[: 2 * section], rest[2 * section]
        table = species_rows(species_ref, pieces).astype(BF16)
        chosen = swapped(section_list(lists_ref, section))
        out_ref[...] = dot(table, onehot_of(chosen, table.shape[1]))

    return kernel


def first_kernel(species_ref, lists_ref, out_ref, species_copy, lists_copy):
    pick_species(0)(species_ref, lists_ref, out_ref)
    species_copy[...] = species_ref[...]
    lists_copy[...] = lists_ref[...]


def send_rows(lists_ref, section, table, low_ref, high_ref):
    chosen = dot_first(onehot_of(section_list(lists_ref, section), table.shape[0]), table)
    high_ref[...] = chosen[:64].astype(BF16)
    low_ref[...] = chosen[64:].astype(BF16)


def pick_rows(section):
    def kernel(lists_ref, *rest):
        table = jnp.concatenate([piece[...] for piece in rest[:-2]], axis=0)
        send_rows(lists_ref, section, table, *rest[-2:])

    return kernel


def by_group(x):
    rows, lanes = x.shape
    row = lax.broadcasted_iota(jnp.int32, x.shape, 0)
    block = lax.broadcasted_iota(jnp.int32, x.shape, 1) >> 3
    step = 1
    while step < rows:
        up = pltpu.roll(pltpu.roll(x, 8 * step, axis=1), rows - step, axis=0)
        down = pltpu.roll(pltpu.roll(x, lanes - 8 * step, axis=1), step, axis=0)
        moved = jnp.where((block & step) != 0, up, down)
        x = jnp.where(((row ^ block) & step) != 0, moved, x)
        step *= 2
    return x


def store_rows(ref, rows):
    for n, row in enumerate(rows):
        size = row.shape[0]
        for tile in range(ref.shape[0]):
            ref[tile, n * size : (n + 1) * size, :] = row[:, tile * 128 : (tile + 1) * 128]


def spread(ref, row):
    parts = [ref[tile, pl.ds(row, 8, stride=0), :] for tile in range(ref.shape[0])]
    return jnp.concatenate(parts, axis=1)


def basis_rows(ref, slot, slots):
    parts = [ref[tile, pl.ds(slot, BASIS, stride=slots), :] for tile in range(ref.shape[0])]
    return jnp.concatenate(parts, axis=1)


def radial_rows(first, hid_ref, out_ref, radial_ref):
    def step(g, carry):
        radial_ref[g] = dot(hid_ref[first + g], out_ref[...])
        return carry

    lax.fori_loop(0, radial_ref.shape[0], step, 0, unroll=2)


def geometry_kernel(
    vec_ref, count_ref, index_ref, y_ref, phi_ref, where_ref
):
    slots, atoms = index_ref.shape
    live = lax.broadcasted_iota(jnp.int32, (slots, atoms), 0) < count_ref[...]
    weight = by_group(jnp.where(live, 0.25, 0.0))
    vx, vy, vz = (by_group(vec_ref[n]) for n in range(3))
    rows, radius, inverse = harmonics(vx, vy, vz, weight)
    store_rows(y_ref, rows)
    store_rows(phi_ref, radial_basis(radius, inverse, 5.0))
    where_ref[...] = by_group(index_ref[...].astype(F32)).astype(jnp.int32)


def first_radial_kernel(
    in1_ref, in2_ref, out1_ref, out2_ref, emb_ref, msg_ref, phi_ref,
    hid_ref, rows_ref, wide1_ref, wide2_ref, radial_ref,
):
    rows_ref[...] = dot(emb_ref[...], msg_ref[...]).astype(BF16)
    empty = jnp.zeros((64, 512), BF16)
    wide1_ref[:64, :], wide1_ref[64:, :] = out1_ref[...], empty
    wide2_ref[:64, :], wide2_ref[64:, :] = empty, out2_ref[...]
    groups = hid_ref.shape[0]
    into = jnp.concatenate([in1_ref[...], in2_ref[...]], axis=1)
    for g in range(groups):
        value = dot_first(basis_rows(phi_ref, g, groups).astype(BF16), into)
        hid_ref[g] = (value / (1.0 + jnp.exp(-value))).astype(BF16)
    radial_rows(0, hid_ref, wide1_ref, radial_ref)


def radial_kernel(first):
    def kernel(hid_ref, out_ref, radial_ref):
        radial_rows(first, hid_ref, out_ref, radial_ref)

    return kernel


def last_radial_kernel(first):
    def kernel(hid_ref, out_ref, dec_ref, radial_ref, blocks_ref):
        radial_rows(first, hid_ref, out_ref, radial_ref)
        column = lax.broadcasted_iota(jnp.int32, (8, 128), 1)
        repeat = (column & 7) == lax.broadcasted_iota(jnp.int32, (8, 128), 0)
        repeat = jnp.where(repeat, 1.0, 0.0).astype(BF16)
        group = lax.broadcasted_iota(jnp.int32, (128, 128), 1) >> 3
        for degree in range(4):
            wide = dot_first(dec_ref[degree], repeat)
            for m in range(degree * degree, (degree + 1) * (degree + 1)):
                block = jnp.where(group == m, wide, 0.0).astype(BF16)
                blocks_ref[m * 128 : (m + 1) * 128, :] = block

    return kernel


def group_sums(g, groups, radial, y_ref, picked):
    own = (lax.broadcasted_iota(jnp.int32, (8, 256), 1) & 7) == lax.broadcasted_iota(
        jnp.int32, (8, 256), 0
    )
    twice = jnp.concatenate([picked, picked], axis=1)
    sums = []
    for degrees, first, last in (((0, 1), 0, 4), ((2, 3), 4, 16)):
        lane = degrees[0] * 128
        weighted = (radial[:, lane : lane + 256] * twice).astype(BF16)
        angular = [jnp.where(own, spread(y_ref, m * groups + g), 0.0) for m in range(first, last)]
        total = dot(jnp.concatenate(angular, axis=0).astype(BF16), weighted)
        for m in range(first, last):
            side = 0 if m < (degrees[0] + 1) ** 2 else 128
            sums.append(total[8 * (m - first) : 8 * (m - first + 1), side : side + 128])
    return sums


def each_pair(radials, pair):
    first = 0
    for radial in radials:

        def step(j, carry, first=first, radial=radial):
            groups = [(first + 2 * j + n, radial.at[2 * j + n]) for n in range(2)]
            pair(pl.multiple_of((first + 2 * j) * 8, 16), groups)
            return carry

        lax.fori_loop(0, radial.shape[0] // 2, step, 0, unroll=4)
        first += radial.shape[0]


def layer_one_kernel(
    species_ref, xl, xh, yl, yh, zl, zh, where_ref, y_ref, radial_a, radial_b, rows_ref, emb_ref,
    self_ref, mix_ref, msg2_ref, lists_ref, next_ref, low_ref, high_ref, onehot, feats,
):
    groups, edges = where_ref.shape
    atoms = species_ref.shape[1]
    table = species_rows(species_ref, (xl, xh, yl, yh, zl, zh))
    blocks = []
    for lane in range(0, edges, 128):
        column = []
        for row in range(0, groups, 8):
            where = swapped(where_ref[row : row + 8, lane : lane + 128])
            found = jnp.zeros((8, 128), F32)
            for b in range(5):
                part = jnp.take_along_axis(table[:, b * 128 : (b + 1) * 128], where & 127, axis=1)
                found = jnp.where((where >> 7) == b, part, found)
            column.append(found)
        blocks.append(jnp.concatenate(column, axis=0))
    kinds = jnp.concatenate(blocks, axis=1).T.astype(BF16)
    lane_group = lax.broadcasted_iota(jnp.int32, (groups, 8 * groups), 1) >> 3
    widen = lane_group == lax.broadcasted_iota(jnp.int32, (groups, 8 * groups), 0)
    kinds = dot(kinds, jnp.where(widen, 1.0, 0.0).astype(BF16))
    kind_of_lane = lax.broadcasted_iota(jnp.int32, kinds.shape, 1) & 7
    onehot[...] = jnp.where(kinds == kind_of_lane.astype(F32), 1.0, 0.0).astype(BF16)
    tall = jnp.concatenate([rows_ref[...].astype(F32)] * groups, axis=0)
    row_group = lax.broadcasted_iota(jnp.int32, tall.shape, 0) >> 3

    def pair(row, members):
        parts = []
        own_rows = [jnp.where(row_group == g, tall, 0.0) for g, _ in members]
        found = dot(onehot[...], jnp.concatenate(own_rows, axis=1).astype(BF16))
        for n, (g, radial) in enumerate(members):
            sums = group_sums(g, groups, radial, y_ref, found[:, 128 * n : 128 * (n + 1)])
            part = [sums[0]]
            for degree in (1, 2, 3):
                part.append(sum(v * v for v in sums[degree * degree : (degree + 1) ** 2]))
            parts.append(jnp.concatenate(part, axis=1))
        feats[pl.ds(row, 16), :] = jnp.concatenate(parts, axis=0).astype(BF16)

    each_pair((radial_a, radial_b), pair)
    kind_ids = lax.broadcasted_iota(jnp.int32, (8, atoms), 0).astype(F32)
    own = jnp.where(table[:, :atoms] == kind_ids, 1.0, 0.0).astype(BF16)
    start = dot_first(own, emb_ref[...]).astype(BF16)
    mixed = dot(start, self_ref[...]) + dot(feats[...], mix_ref[...])
    hidden = (mixed / (1.0 + jnp.exp(-mixed))).astype(BF16)
    message = dot(hidden, msg2_ref[...]).astype(BF16)
    next_ref[...] = message
    send_rows(lists_ref, 0, message, low_ref, high_ref)


def layer_two_kernel(
    own_ref, xl, xh, yl, yh, zl, zh, where_ref, y_ref, radial_a, radial_b, radial_c, blocks_ref,
    lists_ref, coeff_ref, low_ref, high_ref, feats, wide, index,
):
    groups, edges = where_ref.shape
    pieces = [piece[...].astype(F32) for piece in (own_ref, xl, xh, yl, yh, zl, zh)]
    table = jnp.concatenate(pieces + [jnp.zeros((128, 128), F32)], axis=0)
    table = jnp.concatenate([table[256 * n : 256 * (n + 1)] for n in range(3)], axis=1)
    wide[...] = table[:, :384].astype(BF16)
    halves = (where_ref[...] & 255, where_ref[...] >> 8)
    index[...] = jnp.concatenate([half.astype(F32).T for half in halves], axis=1).astype(BF16)
    source = lax.broadcasted_iota(jnp.int32, (2 * groups, 512), 0)
    target = lax.broadcasted_iota(jnp.int32, (2 * groups, 512), 1) >> 7
    low_ids = lax.broadcasted_iota(jnp.int32, (edges, 128), 1).astype(F32)

    def pair(row, members):
        parts, onehots = [], []
        first = members[0][0]
        picks = source == first + (target & 1) + jnp.where(target < 2, 0, groups)
        spread_index = dot(index[...], jnp.where(picks, 1.0, 0.0).astype(BF16))
        for n in range(2):
            low = spread_index[:, 128 * n : 128 * (n + 1)]
            sides = [jnp.where(low == low_ids + 128.0 * side, 1.0, 0.0) for side in range(2)]
            onehots.append(jnp.concatenate(sides, axis=1))
        found = dot(jnp.concatenate(onehots, axis=0).astype(BF16), wide[...])
        for n, (g, radial) in enumerate(members):
            high = spread_index[:, 256 + 128 * n : 384 + 128 * n]
            mine = found[edges * n : edges * (n + 1)]
            picked = jnp.where(high < 0.5, mine[:, :128], mine[:, 128:256])
            picked = jnp.where(high < 1.5, picked, mine[:, 256:])
            sums = group_sums(g, groups, radial, y_ref, picked)
            parts.append(jnp.concatenate(sums, axis=1))
        feats[pl.ds(row, 16), :] = jnp.concatenate(parts, axis=0).astype(BF16)

    each_pair((radial_a, radial_b, radial_c), pair)
    coeffs = dot(feats[...], blocks_ref[...]).astype(BF16)
    coeff_ref[...] = coeffs
    send_rows(lists_ref, 0, coeffs, low_ref, high_ref)


SWAPS = ((2, 1), (1, 1), (2, 0), (1, 0))


def partner_slot(distance, first):
    ahead = (lax.axis_index("gy") // distance) % 2 == first
    return jnp.where(ahead, 2 + distance, 2 - distance)


def brick_kernel(list_ref, *rest):
    pieces, outs, chosen = rest[:7], rest[7:12], rest[12]
    table = jnp.concatenate([piece[...] for piece in pieces], axis=0)
    chosen[...] = dot_first(onehot_of(list_ref[...], table.shape[0]), table)
    for swap, out in zip(SWAPS, outs):
        first = pl.multiple_of(partner_slot(*swap) * 32, 32)
        out[...] = chosen[pl.ds(first, 32), :].astype(BF16)
    outs[4][...] = chosen[64:96].astype(BF16)


def probe_kernel(
    column, list_ref, count_ref, vec_ref, index_ref, y_ref, phi_ref, where_ref, nearby_ref
):
    slots, probes = index_ref.shape
    live = lax.broadcasted_iota(jnp.int32, (slots, probes), 0) < count_ref[...]
    weight = jnp.where(live, 0.125, 0.0)
    rows, radius, inverse = harmonics(vec_ref[0], vec_ref[1], vec_ref[2], weight)
    store_rows(y_ref, rows)
    store_rows(phi_ref, radial_basis(radius, inverse, 4.0))
    here = lax.axis_index("gy")
    index = index_ref[...]
    source = (index >> 5) - here + 2
    source = jnp.where(source < 0, source + column, source)
    source = jnp.where(source >= column, source - column, source)
    where_ref[...] = source * 32 + (index & 31)
    targets = list_ref.shape[1]
    start = (2 - here) * (targets // column)
    start = jnp.where(start < 0, start + targets, start)
    turned = pltpu.roll(jnp.broadcast_to(list_ref[...], (8, targets)), start, axis=1)
    nearby_ref[...] = turned[:1, :256]


def density_kernel(p0, p1, p2, p3, p4, where_ref, y, phi, out_ref, table):
    slots, probes = where_ref.shape
    table[160:, :] = jnp.zeros((96, 128), F32)
    table[64:96, :] = p4[...].astype(F32)
    for swap, piece in zip(SWAPS, (p0, p1, p2, p3)):
        first = pl.multiple_of(partner_slot(*swap) * 32, 32)
        table[pl.ds(first, 32), :] = piece[...].astype(F32)
    rows_t = table[...].T[:, :160].astype(BF16)

    def slot(k, total):
        picked = dot(rows_t, onehot_of(where_ref[pl.ds(k, 1), :], 160))
        part = jnp.zeros((8, probes), F32)
        for m in range(16):
            part = part + spread(y, m * slots + k) * picked[m * 8 : (m + 1) * 8]
        return total + part * basis_rows(phi, k, slots)

    total = lax.fori_loop(0, slots, slot, jnp.zeros((8, probes), F32), unroll=4)
    out_ref[...] = jnp.sum(total, axis=0, keepdims=True)


def shifted(block, axis, step):
    size = lax.axis_size(axis)
    return lax.ppermute(block, axis, [(i, (i + step) % size) for i in range(size)])


def swapped_with(block, distance, first):
    size = lax.axis_size("gy")
    pairs = []
    for low in range(size):
        if (low // distance) % 2 == first:
            high = (low + distance) % size
            pairs += [(low, high), (high, low)]
    return lax.ppermute(block, "gy", sorted(pairs))


def extend(rows, low, high, lists, fillers):
    half = jax.ShapeDtypeStruct((64, 128), BF16)
    pieces, made, begin = [], [], rows
    for section, axis in enumerate(("gx", "gy", "gz")):
        if section:
            done = made[-1][-1:] if made[-1] else ()
            low, high = call(
                pick_rows(section), (half, half), (lists, rows, *pieces), after=done
            )
            begin = low
        pieces += [shifted(low, axis, 1), shifted(high, axis, -1)]
        made.append(fillers[section](made, begin) if fillers[section] else ())
    return pieces, made


def shards(
    species, neighbour_index, neighbour_count, edge_vectors, ghost_send, brick_send, probe_index,
    probe_count, probe_vectors, embedding, message_one, radial_in_one, radial_out_one, self_mix,
    basis_mix, message_two, radial_in_two, radial_out_two, decoder,
):
    slots, atoms = neighbour_index.shape[3:]
    probes = probe_index.shape[-1]
    kinds = species.reshape(1, atoms)
    lists = ghost_send.reshape(1, 384)
    shape = jax.ShapeDtypeStruct
    half = shape((64, 128), BF16)
    column = lax.axis_size("gy")

    def both(block, axis):
        return [shifted(block, axis, 1), shifted(block, axis, -1)]

    row = shape((8, 128), F32)
    hidden = shape((slots, atoms, 128), BF16)
    wide = shape((128, 512), BF16)

    def radial(count):
        return shape((count, atoms, 512), F32)

    chosen, kinds, lists = call(
        first_kernel,
        (row, shape(kinds.shape, jnp.int32), shape(lists.shape, jnp.int32)),
        (),
        staged=(kinds, lists),
    )
    ghosts = both(chosen, "gx")
    angular, phi, where = call(
        geometry_kernel,
        (
            shape((2, 16 * slots, 128), F32),
            shape((2, BASIS * slots, 128), F32),
            shape((slots, atoms), jnp.int32),
        ),
        (),
        staged=(
            edge_vectors.reshape(3, slots, atoms),
            neighbour_count.reshape(1, atoms),
            neighbour_index.reshape(slots, atoms),
        ),
        after=(chosen,),
    )
    chosen = call(pick_species(1), row, (kinds, lists, *ghosts), after=(where,))
    ghosts += both(chosen, "gy")
    hidden_both, rows, wide_one, wide_two, radial_a = call(
        first_radial_kernel,
        (hidden, shape((8, 128), BF16), wide, wide, radial(8)),
        (phi,),
        limit=20,
        staged=(
            radial_in_one,
            radial_in_two,
            radial_out_one,
            radial_out_two,
            embedding,
            message_one,
        ),
        after=(chosen,),
    )
    chosen = call(pick_species(2), row, (kinds, lists, *ghosts), after=(radial_a,))
    ghosts += both(chosen, "gz")
    radial_b = call(
        radial_kernel(8), radial(24), (hidden_both, wide_one), limit=30, after=(chosen,)
    )
    second = call(
        layer_one_kernel,
        (shape((atoms, 128), BF16), half, half),
        (kinds, *ghosts, where, angular, radial_a, radial_b, rows, embedding, self_mix,
         basis_mix, message_two, lists),
        [pltpu.VMEM((atoms, 256), BF16), pltpu.VMEM((atoms, 512), BF16)],
        limit=16,
    )
    pieces, made = extend(
        *second,
        lists,
        (
            lambda made, begin: (
                call(
                    radial_kernel(0),
                    radial(8),
                    (hidden_both, wide_two),
                    limit=20,
                    after=(begin,),
                ),
            ),
            lambda made, begin: (
                call(
                    radial_kernel(8),
                    radial(16),
                    (hidden_both, wide_two),
                    limit=20,
                    after=(begin,),
                ),
            ),
            lambda made, begin: call(
                last_radial_kernel(24),
                (radial(8), shape((2048, 128), BF16)),
                (hidden_both, wide_two, decoder.transpose(0, 2, 1)),
                limit=20,
                after=(begin,),
            ),
        ),
    )
    coeffs = call(
        layer_two_kernel,
        (shape((atoms, 128), BF16), half, half),
        (second[0], *pieces, where, angular, made[0][0], made[1][0], *made[2], lists),
        [
            pltpu.VMEM((atoms, 2048), BF16),
            pltpu.VMEM((256, 384), BF16),
            pltpu.VMEM((atoms, 2 * slots), BF16),
        ],
        limit=16,
    )
    pieces, made = extend(
        *coeffs,
        lists,
        (
            lambda made, begin: call(
                functools.partial(probe_kernel, column),
                (
                    shape((probes // 128, 16 * slots, 128), F32),
                    shape((probes // 128, BASIS * slots, 128), F32),
                    shape((slots, probes), jnp.int32),
                    shape((1, 256), jnp.int32),
                ),
                (
                    brick_send.reshape(1, -1),
                    probe_count.reshape(1, probes),
                    probe_vectors.reshape(3, slots, probes),
                    probe_index.reshape(slots, probes),
                ),
                after=(begin,),
            ),
            None,
            None,
        ),
    )
    probe_y, probe_phi, probe_where, nearby = made[0]
    sent = call(
        brick_kernel,
        [shape((32, 128), BF16)] * 5,
        (nearby, coeffs[0], *pieces),
        [pltpu.VMEM((256, 128), F32)],
    )
    pieces = [swapped_with(sent[n], *SWAPS[n]) for n in (3, 2, 1, 0)][::-1] + [sent[4]]
    density = call(
        density_kernel,
        shape((1, probes), F32),
        (*pieces, probe_where, probe_y, probe_phi),
        [pltpu.VMEM((256, 128), F32)],
    )
    return density.reshape(1, 1, 1, probes)


def solution(mesh):
    domain = ("gx", "gy", "gz")
    placed = tuple(P(*domain) for _ in range(9)) + tuple(P() for _ in range(10))
    return jax.shard_map(
        shards, mesh=mesh, in_specs=placed, out_specs=P(*domain), check_vma=False
    )
```

```python
import functools
import math

import jax
import jax.numpy as jnp
from jax import lax
from jax.experimental import pallas as pl
from jax.experimental.pallas import tpu as pltpu
from jax.sharding import PartitionSpec as P

BASIS = 8
F32 = jnp.float32
BF16 = jnp.bfloat16
VMEM = pl.BlockSpec(memory_space=pltpu.VMEM)
HBM = pl.BlockSpec(memory_space=pltpu.HBM)
ANY = pl.BlockSpec(memory_space=pl.ANY)


def call(kernel, out_shape, operands, scratch=(), limit=8, staged=(), after=()):
    first, last = len(staged), len(staged) + len(operands)

    def body(*refs):
        if not staged:
            return kernel(*refs[:last], *refs[last + len(after) :])
        buffers, arrived = refs[-1 - first : -1], refs[-1]
        copies = [
            pltpu.make_async_copy(source, target, arrived.at[n])
            for n, (source, target) in enumerate(zip(refs, buffers))
        ]
        for copy in copies:
            copy.start()
        for copy in copies:
            copy.wait()
        kernel(*buffers, *refs[first:last], *refs[last + len(after) : -1 - first])

    room = [pltpu.VMEM(x.shape, x.dtype) for x in staged]
    if staged:
        room.append(pltpu.SemaphoreType.DMA((first,)))
    held = [pltpu.with_memory_space_constraint(x, pltpu.HBM) for x in staged]
    return pl.pallas_call(
        body,
        out_shape=out_shape,
        in_specs=[HBM] * first + [VMEM] * len(operands) + [ANY] * len(after),
        out_specs=jax.tree.map(lambda _: VMEM, out_shape),
        scratch_shapes=[*scratch, *room],
        compiler_params=pltpu.CompilerParams(vmem_limit_bytes=limit << 20),
        cost_estimate=pl.CostEstimate(flops=0, bytes_accessed=1 << 20, transcendentals=0),
    )(*held, *operands, *after)


def dot(a, b):
    return jnp.dot(a, b, preferred_element_type=F32)


def dot_first(a, b):
    return lax.dot_general(a, b, (((0,), (0,)), ((), ())), preferred_element_type=F32)


def harmonics(vx, vy, vz, weight):
    radius = jnp.sqrt(vx * vx + vy * vy + vz * vz)
    inverse = 1.0 / radius
    x, y, z = vx * inverse, vy * inverse, vz * inverse
    xx, yy, zz = x * x, y * y, z * z
    r3, r15, r5, r105, r7 = (math.sqrt(v) for v in (3.0, 15.0, 5.0, 105.0, 7.0))
    outer, inner = math.sqrt(35.0 / 8.0), math.sqrt(21.0 / 8.0)
    rows = [
        jnp.ones_like(x),
        r3 * x,
        r3 * y,
        r3 * z,
        r15 * x * y,
        r15 * y * z,
        0.5 * r5 * (3.0 * zz - 1.0),
        r15 * x * z,
        0.5 * r15 * (xx - yy),
        outer * y * (3.0 * xx - yy),
        r105 * x * y * z,
        inner * y * (5.0 * zz - 1.0),
        0.5 * r7 * z * (5.0 * zz - 3.0),
        inner * x * (5.0 * zz - 1.0),
        0.5 * r105 * z * (xx - yy),
        outer * x * (xx - 3.0 * yy),
    ]
    return [row * weight for row in rows], radius, inverse


def radial_basis(radius, inverse, cutoff):
    u = radius * (1.0 / cutoff)
    u2 = u * u
    envelope = 1.0 + u2 * u2 * u2 * (-28.0 + u * (48.0 - 21.0 * u))
    scale = math.sqrt(2.0 / cutoff) * inverse * envelope
    angle = radius * (math.pi / cutoff)
    before, now = jnp.zeros_like(angle), jnp.sin(angle)
    twice = 2.0 * jnp.cos(angle)
    rows = []
    for _ in range(BASIS):
        rows.append(now * scale)
        before, now = now, twice * now - before
    return rows


def sections(arrays):
    return jnp.where(lax.broadcasted_iota(jnp.int32, (8, 128), 1) < 64, arrays[1], arrays[0])


def swapped(index):
    return jnp.where(index >= 256, index ^ 64, index)


def species_rows(species_ref, pieces):
    parts = [jnp.broadcast_to(species_ref[...].astype(F32), (8, 256))]
    for first in range(0, len(pieces), 2):
        parts.append(sections((pieces[first][...], pieces[first + 1][...])))
    return jnp.concatenate(parts, axis=1)


def onehot_of(chosen, rows):
    row_ids = lax.broadcasted_iota(jnp.int32, (rows, chosen.shape[1]), 0)
    return jnp.where(row_ids == chosen, 1.0, 0.0).astype(BF16)


def section_list(lists_ref, section):
    return lists_ref[:, section * 128 : (section + 1) * 128]


def pick_species(section):
    def kernel(species_ref, lists_ref, *rest):
        pieces, out_ref = rest[: 2 * section], rest[2 * section]
        table = species_rows(species_ref, pieces).astype(BF16)
        chosen = swapped(section_list(lists_ref, section))
        out_ref[...] = dot(table, onehot_of(chosen, table.shape[1]))

    return kernel


def first_kernel(species_ref, lists_ref, out_ref, species_copy, lists_copy):
    pick_species(0)(species_ref, lists_ref, out_ref)
    species_copy[...] = species_ref[...]
    lists_copy[...] = lists_ref[...]


def send_rows(lists_ref, section, table, low_ref, high_ref):
    chosen = dot_first(onehot_of(section_list(lists_ref, section), table.shape[0]), table)
    high_ref[...] = chosen[:64].astype(BF16)
    low_ref[...] = chosen[64:].astype(BF16)


def pick_rows(section):
    def kernel(lists_ref, *rest):
        table = jnp.concatenate([piece[...] for piece in rest[:-2]], axis=0)
        send_rows(lists_ref, section, table, *rest[-2:])

    return kernel


def by_group(x):
    rows, lanes = x.shape
    row = lax.broadcasted_iota(jnp.int32, x.shape, 0)
    block = lax.broadcasted_iota(jnp.int32, x.shape, 1) >> 3
    step = 1
    while step < rows:
        up = pltpu.roll(pltpu.roll(x, 8 * step, axis=1), rows - step, axis=0)
        down = pltpu.roll(pltpu.roll(x, lanes - 8 * step, axis=1), step, axis=0)
        moved = jnp.where((block & step) != 0, up, down)
        x = jnp.where(((row ^ block) & step) != 0, moved, x)
        step *= 2
    return x


def store_rows(ref, rows):
    for n, row in enumerate(rows):
        size = row.shape[0]
        for tile in range(ref.shape[0]):
            ref[tile, n * size : (n + 1) * size, :] = row[:, tile * 128 : (tile + 1) * 128]


def spread(ref, row):
    parts = [ref[tile, pl.ds(row, 8, stride=0), :] for tile in range(ref.shape[0])]
    return jnp.concatenate(parts, axis=1)


def basis_rows(ref, slot, slots):
    parts = [ref[tile, pl.ds(slot, BASIS, stride=slots), :] for tile in range(ref.shape[0])]
    return jnp.concatenate(parts, axis=1)


def radial_rows(first, hid_ref, out_ref, radial_ref):
    def step(g, carry):
        radial_ref[g] = dot(hid_ref[first + g], out_ref[...])
        return carry

    lax.fori_loop(0, radial_ref.shape[0], step, 0, unroll=4)


def geometry_kernel(
    vec_ref, count_ref, index_ref, y_ref, phi_ref, where_ref
):
    slots, atoms = index_ref.shape
    live = lax.broadcasted_iota(jnp.int32, (slots, atoms), 0) < count_ref[...]
    weight = by_group(jnp.where(live, 0.25, 0.0))
    vx, vy, vz = (by_group(vec_ref[n]) for n in range(3))
    rows, radius, inverse = harmonics(vx, vy, vz, weight)
    coarse = [row.astype(BF16).astype(F32) for row in rows]
    store_rows(y_ref, coarse + [row - near for row, near in zip(rows, coarse)])
    store_rows(phi_ref, radial_basis(radius, inverse, 5.0))
    where_ref[...] = by_group(index_ref[...].astype(F32)).astype(jnp.int32)


def first_radial_kernel(
    in1_ref, in2_ref, out1_ref, out2_ref, emb_ref, msg_ref, phi_ref,
    hid_ref, rows_ref, wide1_ref, wide2_ref, radial_ref,
):
    rows_ref[...] = dot(emb_ref[...], msg_ref[...]).astype(BF16)
    empty = jnp.zeros((64, 512), BF16)
    wide1_ref[:64, :], wide1_ref[64:, :] = out1_ref[...], empty
    wide2_ref[:64, :], wide2_ref[64:, :] = empty, out2_ref[...]
    groups = hid_ref.shape[0]
    into = jnp.concatenate([in1_ref[...], in2_ref[...]], axis=1)
    for g in range(groups):
        value = dot_first(basis_rows(phi_ref, g, groups).astype(BF16), into)
        hid_ref[g] = (value / (1.0 + jnp.exp(-value))).astype(BF16)
    radial_rows(0, hid_ref, wide1_ref, radial_ref)


def radial_kernel(first):
    def kernel(hid_ref, out_ref, radial_ref):
        radial_rows(first, hid_ref, out_ref, radial_ref)

    return kernel


def last_radial_kernel(first):
    def kernel(hid_ref, out_ref, dec_ref, radial_ref, blocks_ref):
        radial_rows(first, hid_ref, out_ref, radial_ref)
        column = lax.broadcasted_iota(jnp.int32, (8, 128), 1)
        repeat = (column & 7) == lax.broadcasted_iota(jnp.int32, (8, 128), 0)
        repeat = jnp.where(repeat, 1.0, 0.0).astype(BF16)
        group = lax.broadcasted_iota(jnp.int32, (128, 128), 1) >> 3
        for degree in range(4):
            wide = dot_first(dec_ref[degree], repeat)
            for m in range(degree * degree, (degree + 1) * (degree + 1)):
                block = jnp.where(group == m, wide, 0.0).astype(BF16)
                blocks_ref[m * 128 : (m + 1) * 128, :] = block

    return kernel


def group_sums(g, groups, radial, y_ref, picked):
    own = (lax.broadcasted_iota(jnp.int32, (8, 256), 1) & 7) == lax.broadcasted_iota(
        jnp.int32, (8, 256), 0
    )
    twice = jnp.concatenate([picked, picked], axis=1)
    sums = []
    for degrees, first, last in (((0, 1), 0, 4), ((2, 3), 4, 16)):
        lane = degrees[0] * 128
        weighted = (radial[:, lane : lane + 256] * twice).astype(BF16)
        angular = [
            jnp.where(own, spread(y_ref, (m + part) * groups + g), 0.0)
            for part in (0, 16)
            for m in range(first, last)
        ]
        total = dot(jnp.concatenate(angular, axis=0).astype(BF16), weighted)
        total = total[: 8 * (last - first)] + total[8 * (last - first) :]
        for m in range(first, last):
            side = 0 if m < (degrees[0] + 1) ** 2 else 128
            sums.append(total[8 * (m - first) : 8 * (m - first + 1), side : side + 128])
    return sums


def each_pair(radials, pair):
    first = 0
    for radial in radials:

        def step(j, carry, first=first, radial=radial):
            groups = [(first + 2 * j + n, radial.at[2 * j + n]) for n in range(2)]
            pair(pl.multiple_of((first + 2 * j) * 8, 16), groups)
            return carry

        lax.fori_loop(0, radial.shape[0] // 2, step, 0, unroll=4)
        first += radial.shape[0]


def layer_one_kernel(
    species_ref, xl, xh, yl, yh, zl, zh, where_ref, y_ref, radial_a, radial_b, rows_ref, emb_ref,
    self_ref, mix_ref, msg2_ref, lists_ref, next_ref, low_ref, high_ref, onehot, feats,
):
    groups, edges = where_ref.shape
    atoms = species_ref.shape[1]
    table = species_rows(species_ref, (xl, xh, yl, yh, zl, zh))
    blocks = []
    for lane in range(0, edges, 128):
        column = []
        for row in range(0, groups, 8):
            where = swapped(where_ref[row : row + 8, lane : lane + 128])
            found = jnp.zeros((8, 128), F32)
            for b in range(5):
                part = jnp.take_along_axis(table[:, b * 128 : (b + 1) * 128], where & 127, axis=1)
                found = jnp.where((where >> 7) == b, part, found)
            column.append(found)
        blocks.append(jnp.concatenate(column, axis=0))
    kinds = jnp.concatenate(blocks, axis=1).T.astype(BF16)
    lane_group = lax.broadcasted_iota(jnp.int32, (groups, 8 * groups), 1) >> 3
    widen = lane_group == lax.broadcasted_iota(jnp.int32, (groups, 8 * groups), 0)
    kinds = dot(kinds, jnp.where(widen, 1.0, 0.0).astype(BF16))
    kind_of_lane = lax.broadcasted_iota(jnp.int32, kinds.shape, 1) & 7
    onehot[...] = jnp.where(kinds == kind_of_lane.astype(F32), 1.0, 0.0).astype(BF16)
    tall = jnp.concatenate([rows_ref[...].astype(F32)] * groups, axis=0)
    row_group = lax.broadcasted_iota(jnp.int32, tall.shape, 0) >> 3

    def pair(row, members):
        parts = []
        own_rows = [jnp.where(row_group == g, tall, 0.0) for g, _ in members]
        found = dot(onehot[...], jnp.concatenate(own_rows, axis=1).astype(BF16))
        for n, (g, radial) in enumerate(members):
            sums = group_sums(g, groups, radial, y_ref, found[:, 128 * n : 128 * (n + 1)])
            part = [sums[0]]
            for degree in (1, 2, 3):
                part.append(sum(v * v for v in sums[degree * degree : (degree + 1) ** 2]))
            parts.append(jnp.concatenate(part, axis=1))
        feats[pl.ds(row, 16), :] = jnp.concatenate(parts, axis=0).astype(BF16)

    each_pair((radial_a, radial_b), pair)
    kind_ids = lax.broadcasted_iota(jnp.int32, (8, atoms), 0).astype(F32)
    own = jnp.where(table[:, :atoms] == kind_ids, 1.0, 0.0).astype(BF16)
    start = dot_first(own, emb_ref[...]).astype(BF16)
    mixed = dot(start, self_ref[...]) + dot(feats[...], mix_ref[...])
    hidden = (mixed / (1.0 + jnp.exp(-mixed))).astype(BF16)
    message = dot(hidden, msg2_ref[...]).astype(BF16)
    next_ref[...] = message
    send_rows(lists_ref, 0, message, low_ref, high_ref)


def layer_two_kernel(
    own_ref, xl, xh, yl, yh, zl, zh, where_ref, y_ref, radial_a, radial_b, radial_c, blocks_ref,
    lists_ref, coeff_ref, low_ref, high_ref, feats, wide, index,
):
    groups, edges = where_ref.shape
    pieces = [piece[...].astype(F32) for piece in (own_ref, xl, xh, yl, yh, zl, zh)]
    table = jnp.concatenate(pieces + [jnp.zeros((128, 128), F32)], axis=0)
    table = jnp.concatenate([table[256 * n : 256 * (n + 1)] for n in range(3)], axis=1)
    wide[...] = table[:, :384].astype(BF16)
    halves = (where_ref[...] & 255, where_ref[...] >> 8)
    index[...] = jnp.concatenate([half.astype(F32).T for half in halves], axis=1).astype(BF16)
    source = lax.broadcasted_iota(jnp.int32, (2 * groups, 512), 0)
    target = lax.broadcasted_iota(jnp.int32, (2 * groups, 512), 1) >> 7
    low_ids = lax.broadcasted_iota(jnp.int32, (edges, 128), 1).astype(F32)

    def pair(row, members):
        parts, onehots = [], []
        first = members[0][0]
        picks = source == first + (target & 1) + jnp.where(target < 2, 0, groups)
        spread_index = dot(index[...], jnp.where(picks, 1.0, 0.0).astype(BF16))
        for n in range(2):
            low = spread_index[:, 128 * n : 128 * (n + 1)]
            sides = [jnp.where(low == low_ids + 128.0 * side, 1.0, 0.0) for side in range(2)]
            onehots.append(jnp.concatenate(sides, axis=1))
        found = dot(jnp.concatenate(onehots, axis=0).astype(BF16), wide[...])
        for n, (g, radial) in enumerate(members):
            high = spread_index[:, 256 + 128 * n : 384 + 128 * n]
            mine = found[edges * n : edges * (n + 1)]
            picked = jnp.where(high < 0.5, mine[:, :128], mine[:, 128:256])
            picked = jnp.where(high < 1.5, picked, mine[:, 256:])
            sums = group_sums(g, groups, radial, y_ref, picked)
            parts.append(jnp.concatenate(sums, axis=1))
        feats[pl.ds(row, 16), :] = jnp.concatenate(parts, axis=0).astype(BF16)

    each_pair((radial_a, radial_b, radial_c), pair)
    coeffs = dot(feats[...], blocks_ref[...]).astype(BF16)
    coeff_ref[...] = coeffs
    send_rows(lists_ref, 0, coeffs, low_ref, high_ref)


SWAPS = ((2, 1), (1, 1), (2, 0), (1, 0))


def partner_slot(distance, first):
    ahead = (lax.axis_index("gy") // distance) % 2 == first
    return jnp.where(ahead, 2 + distance, 2 - distance)


def brick_kernel(list_ref, *rest):
    pieces, outs, chosen = rest[:7], rest[7:12], rest[12]
    table = jnp.concatenate([piece[...] for piece in pieces], axis=0)
    chosen[...] = dot_first(onehot_of(list_ref[...], table.shape[0]), table)
    for swap, out in zip(SWAPS, outs):
        first = pl.multiple_of(partner_slot(*swap) * 32, 32)
        out[...] = chosen[pl.ds(first, 32), :].astype(BF16)
    outs[4][...] = chosen[64:96].astype(BF16)


def probe_kernel(
    column, list_ref, count_ref, vec_ref, index_ref, y_ref, phi_ref, where_ref, nearby_ref
):
    slots, probes = index_ref.shape
    live = lax.broadcasted_iota(jnp.int32, (slots, probes), 0) < count_ref[...]
    weight = jnp.where(live, 0.125, 0.0)
    rows, radius, inverse = harmonics(vec_ref[0], vec_ref[1], vec_ref[2], weight)
    store_rows(y_ref, rows)
    store_rows(phi_ref, radial_basis(radius, inverse, 4.0))
    here = lax.axis_index("gy")
    index = index_ref[...]
    source = (index >> 5) - here + 2
    source = jnp.where(source < 0, source + column, source)
    source = jnp.where(source >= column, source - column, source)
    where_ref[...] = source * 32 + (index & 31)
    targets = list_ref.shape[1]
    start = (2 - here) * (targets // column)
    start = jnp.where(start < 0, start + targets, start)
    turned = pltpu.roll(jnp.broadcast_to(list_ref[...], (8, targets)), start, axis=1)
    nearby_ref[...] = turned[:1, :256]


def density_kernel(p0, p1, p2, p3, p4, where_ref, y, phi, out_ref, table):
    slots, probes = where_ref.shape
    table[160:, :] = jnp.zeros((96, 128), F32)
    table[64:96, :] = p4[...].astype(F32)
    for swap, piece in zip(SWAPS, (p0, p1, p2, p3)):
        first = pl.multiple_of(partner_slot(*swap) * 32, 32)
        table[pl.ds(first, 32), :] = piece[...].astype(F32)
    rows_t = table[...].T[:, :160].astype(BF16)

    def slot(k, total):
        picked = dot(rows_t, onehot_of(where_ref[pl.ds(k, 1), :], 160))
        part = jnp.zeros((8, probes), F32)
        for m in range(16):
            part = part + spread(y, m * slots + k) * picked[m * 8 : (m + 1) * 8]
        return total + part * basis_rows(phi, k, slots)

    total = lax.fori_loop(0, slots, slot, jnp.zeros((8, probes), F32), unroll=4)
    out_ref[...] = jnp.sum(total, axis=0, keepdims=True)


def shifted(block, axis, step):
    size = lax.axis_size(axis)
    return lax.ppermute(block, axis, [(i, (i + step) % size) for i in range(size)])


def swapped_with(block, distance, first):
    size = lax.axis_size("gy")
    pairs = []
    for low in range(size):
        if (low // distance) % 2 == first:
            high = (low + distance) % size
            pairs += [(low, high), (high, low)]
    return lax.ppermute(block, "gy", sorted(pairs))


def extend(rows, low, high, lists, fillers):
    half = jax.ShapeDtypeStruct((64, 128), BF16)
    pieces, made, begin = [], [], rows
    for section, axis in enumerate(("gx", "gy", "gz")):
        if section:
            done = made[-1][-1:] if made[-1] else ()
            low, high = call(
                pick_rows(section), (half, half), (lists, rows, *pieces), after=done
            )
            begin = low
        pieces += [shifted(low, axis, 1), shifted(high, axis, -1)]
        made.append(fillers[section](made, begin) if fillers[section] else ())
    return pieces, made


def shards(
    species, neighbour_index, neighbour_count, edge_vectors, ghost_send, brick_send, probe_index,
    probe_count, probe_vectors, embedding, message_one, radial_in_one, radial_out_one, self_mix,
    basis_mix, message_two, radial_in_two, radial_out_two, decoder,
):
    slots, atoms = neighbour_index.shape[3:]
    probes = probe_index.shape[-1]
    kinds = species.reshape(1, atoms)
    lists = ghost_send.reshape(1, 384)
    shape = jax.ShapeDtypeStruct
    half = shape((64, 128), BF16)
    column = lax.axis_size("gy")

    def both(block, axis):
        return [shifted(block, axis, 1), shifted(block, axis, -1)]

    row = shape((8, 128), F32)
    hidden = shape((slots, atoms, 128), BF16)
    wide = shape((128, 512), BF16)

    def radial(count):
        return shape((count, atoms, 512), F32)

    chosen, kinds, lists = call(
        first_kernel,
        (row, shape(kinds.shape, jnp.int32), shape(lists.shape, jnp.int32)),
        (),
        staged=(kinds, lists),
    )
    ghosts = both(chosen, "gx")
    angular, phi, where = call(
        geometry_kernel,
        (
            shape((2, 32 * slots, 128), F32),
            shape((2, BASIS * slots, 128), F32),
            shape((slots, atoms), jnp.int32),
        ),
        (),
        staged=(
            edge_vectors.reshape(3, slots, atoms),
            neighbour_count.reshape(1, atoms),
            neighbour_index.reshape(slots, atoms),
        ),
        after=(chosen,),
    )
    chosen = call(pick_species(1), row, (kinds, lists, *ghosts), after=(where,))
    ghosts += both(chosen, "gy")
    hidden_both, rows, wide_one, wide_two, radial_a = call(
        first_radial_kernel,
        (hidden, shape((8, 128), BF16), wide, wide, radial(8)),
        (phi,),
        limit=20,
        staged=(
            radial_in_one,
            radial_in_two,
            radial_out_one,
            radial_out_two,
            embedding,
            message_one,
        ),
        after=(chosen,),
    )
    chosen = call(pick_species(2), row, (kinds, lists, *ghosts), after=(radial_a,))
    ghosts += both(chosen, "gz")
    radial_b = call(
        radial_kernel(8), radial(24), (hidden_both, wide_one), limit=30, after=(chosen,)
    )
    second = call(
        layer_one_kernel,
        (shape((atoms, 128), BF16), half, half),
        (kinds, *ghosts, where, angular, radial_a, radial_b, rows, embedding, self_mix,
         basis_mix, message_two, lists),
        [pltpu.VMEM((atoms, 256), BF16), pltpu.VMEM((atoms, 512), BF16)],
        limit=16,
    )
    pieces, made = extend(
        *second,
        lists,
        (
            lambda made, begin: (
                call(
                    radial_kernel(0),
                    radial(8),
                    (hidden_both, wide_two),
                    limit=20,
                    after=(begin,),
                ),
            ),
            lambda made, begin: (
                call(
                    radial_kernel(8),
                    radial(16),
                    (hidden_both, wide_two),
                    limit=20,
                    after=(begin,),
                ),
            ),
            lambda made, begin: call(
                last_radial_kernel(24),
                (radial(8), shape((2048, 128), BF16)),
                (hidden_both, wide_two, decoder.transpose(0, 2, 1)),
                limit=20,
                after=(begin,),
            ),
        ),
    )
    coeffs = call(
        layer_two_kernel,
        (shape((atoms, 128), BF16), half, half),
        (second[0], *pieces, where, angular, made[0][0], made[1][0], *made[2], lists),
        [
            pltpu.VMEM((atoms, 2048), BF16),
            pltpu.VMEM((256, 384), BF16),
            pltpu.VMEM((atoms, 2 * slots), BF16),
        ],
        limit=16,
    )
    pieces, made = extend(
        *coeffs,
        lists,
        (
            lambda made, begin: call(
                functools.partial(probe_kernel, column),
                (
                    shape((probes // 128, 16 * slots, 128), F32),
                    shape((probes // 128, BASIS * slots, 128), F32),
                    shape((slots, probes), jnp.int32),
                    shape((1, 256), jnp.int32),
                ),
                (
                    brick_send.reshape(1, -1),
                    probe_count.reshape(1, probes),
                    probe_vectors.reshape(3, slots, probes),
                    probe_index.reshape(slots, probes),
                ),
                after=(begin,),
            ),
            None,
            None,
        ),
    )
    probe_y, probe_phi, probe_where, nearby = made[0]
    sent = call(
        brick_kernel,
        [shape((32, 128), BF16)] * 5,
        (nearby, coeffs[0], *pieces),
        [pltpu.VMEM((256, 128), F32)],
    )
    pieces = [swapped_with(sent[n], *SWAPS[n]) for n in (3, 2, 1, 0)][::-1] + [sent[4]]
    density = call(
        density_kernel,
        shape((1, probes), F32),
        (*pieces, probe_where, probe_y, probe_phi),
        [pltpu.VMEM((256, 128), F32)],
    )
    return density.reshape(1, 1, 1, probes)


def solution(mesh):
    domain = ("gx", "gy", "gz")
    placed = tuple(P(*domain) for _ in range(9)) + tuple(P() for _ in range(10))
    return jax.shard_map(
        shards, mesh=mesh, in_specs=placed, out_specs=P(*domain), check_vma=False
    )
```

```python
import functools
import math

import jax
import jax.numpy as jnp
from jax import lax
from jax.experimental import pallas as pl
from jax.experimental.pallas import tpu as pltpu
from jax.sharding import PartitionSpec as P

BASIS = 8
F32 = jnp.float32
BF16 = jnp.bfloat16
VMEM = pl.BlockSpec(memory_space=pltpu.VMEM)
HBM = pl.BlockSpec(memory_space=pltpu.HBM)
ANY = pl.BlockSpec(memory_space=pl.ANY)


def call(kernel, out_shape, operands, scratch=(), limit=8, staged=(), after=()):
    first, last = len(staged), len(staged) + len(operands)

    def body(*refs):
        if not staged:
            return kernel(*refs[:last], *refs[last + len(after) :])
        buffers, arrived = refs[-1 - first : -1], refs[-1]
        copies = [
            pltpu.make_async_copy(source, target, arrived.at[n])
            for n, (source, target) in enumerate(zip(refs, buffers))
        ]
        for copy in copies:
            copy.start()
        for copy in copies:
            copy.wait()
        kernel(*buffers, *refs[first:last], *refs[last + len(after) : -1 - first])

    room = [pltpu.VMEM(x.shape, x.dtype) for x in staged]
    if staged:
        room.append(pltpu.SemaphoreType.DMA((first,)))
    held = [pltpu.with_memory_space_constraint(x, pltpu.HBM) for x in staged]
    return pl.pallas_call(
        body,
        out_shape=out_shape,
        in_specs=[HBM] * first + [VMEM] * len(operands) + [ANY] * len(after),
        out_specs=jax.tree.map(lambda _: VMEM, out_shape),
        scratch_shapes=[*scratch, *room],
        compiler_params=pltpu.CompilerParams(vmem_limit_bytes=limit << 20),
        cost_estimate=pl.CostEstimate(flops=0, bytes_accessed=1 << 20, transcendentals=0),
    )(*held, *operands, *after)


def dot(a, b):
    return jnp.dot(a, b, preferred_element_type=F32)


def dot_first(a, b):
    return lax.dot_general(a, b, (((0,), (0,)), ((), ())), preferred_element_type=F32)


def harmonics(vx, vy, vz, weight):
    radius = jnp.sqrt(vx * vx + vy * vy + vz * vz)
    inverse = 1.0 / radius
    x, y, z = vx * inverse, vy * inverse, vz * inverse
    xx, yy, zz = x * x, y * y, z * z
    r3, r15, r5, r105, r7 = (math.sqrt(v) for v in (3.0, 15.0, 5.0, 105.0, 7.0))
    outer, inner = math.sqrt(35.0 / 8.0), math.sqrt(21.0 / 8.0)
    rows = [
        jnp.ones_like(x),
        r3 * x,
        r3 * y,
        r3 * z,
        r15 * x * y,
        r15 * y * z,
        0.5 * r5 * (3.0 * zz - 1.0),
        r15 * x * z,
        0.5 * r15 * (xx - yy),
        outer * y * (3.0 * xx - yy),
        r105 * x * y * z,
        inner * y * (5.0 * zz - 1.0),
        0.5 * r7 * z * (5.0 * zz - 3.0),
        inner * x * (5.0 * zz - 1.0),
        0.5 * r105 * z * (xx - yy),
        outer * x * (xx - 3.0 * yy),
    ]
    return [row * weight for row in rows], radius, inverse


def radial_basis(radius, inverse, cutoff):
    u = radius * (1.0 / cutoff)
    u2 = u * u
    envelope = 1.0 + u2 * u2 * u2 * (-28.0 + u * (48.0 - 21.0 * u))
    scale = math.sqrt(2.0 / cutoff) * inverse * envelope
    angle = radius * (math.pi / cutoff)
    before, now = jnp.zeros_like(angle), jnp.sin(angle)
    twice = 2.0 * jnp.cos(angle)
    rows = []
    for _ in range(BASIS):
        rows.append(now * scale)
        before, now = now, twice * now - before
    return rows


def sections(arrays):
    return jnp.where(lax.broadcasted_iota(jnp.int32, (8, 128), 1) < 64, arrays[1], arrays[0])


def swapped(index):
    return jnp.where(index >= 256, index ^ 64, index)


def species_rows(species_ref, pieces):
    parts = [jnp.broadcast_to(species_ref[...].astype(F32), (8, 256))]
    for first in range(0, len(pieces), 2):
        parts.append(sections((pieces[first][...], pieces[first + 1][...])))
    return jnp.concatenate(parts, axis=1)


def onehot_of(chosen, rows):
    row_ids = lax.broadcasted_iota(jnp.int32, (rows, chosen.shape[1]), 0)
    return jnp.where(row_ids == chosen, 1.0, 0.0).astype(BF16)


def section_list(lists_ref, section):
    return lists_ref[:, section * 128 : (section + 1) * 128]


def pick_species(section):
    def kernel(species_ref, lists_ref, *rest):
        pieces, out_ref = rest[: 2 * section], rest[2 * section]
        table = species_rows(species_ref, pieces).astype(BF16)
        chosen = swapped(section_list(lists_ref, section))
        out_ref[...] = dot(table, onehot_of(chosen, table.shape[1]))

    return kernel


def first_kernel(species_ref, lists_ref, out_ref, species_copy, lists_copy):
    pick_species(0)(species_ref, lists_ref, out_ref)
    species_copy[...] = species_ref[...]
    lists_copy[...] = lists_ref[...]


def send_rows(lists_ref, section, table, low_ref, high_ref):
    chosen = dot_first(onehot_of(section_list(lists_ref, section), table.shape[0]), table)
    high_ref[...] = chosen[:64].astype(BF16)
    low_ref[...] = chosen[64:].astype(BF16)


def pick_rows(section):
    def kernel(lists_ref, *rest):
        table = jnp.concatenate([piece[...] for piece in rest[:-2]], axis=0)
        send_rows(lists_ref, section, table, *rest[-2:])

    return kernel


def by_group(x):
    rows, lanes = x.shape
    row = lax.broadcasted_iota(jnp.int32, x.shape, 0)
    block = lax.broadcasted_iota(jnp.int32, x.shape, 1) >> 3
    step = 1
    while step < rows:
        up = pltpu.roll(pltpu.roll(x, 8 * step, axis=1), rows - step, axis=0)
        down = pltpu.roll(pltpu.roll(x, lanes - 8 * step, axis=1), step, axis=0)
        moved = jnp.where((block & step) != 0, up, down)
        x = jnp.where(((row ^ block) & step) != 0, moved, x)
        step *= 2
    return x


def store_rows(ref, rows):
    for n, row in enumerate(rows):
        size = row.shape[0]
        for tile in range(ref.shape[0]):
            ref[tile, n * size : (n + 1) * size, :] = row[:, tile * 128 : (tile + 1) * 128]


def spread(ref, row):
    parts = [ref[tile, pl.ds(row, 8, stride=0), :] for tile in range(ref.shape[0])]
    return jnp.concatenate(parts, axis=1)


def basis_rows(ref, slot, slots):
    parts = [ref[tile, pl.ds(slot, BASIS, stride=slots), :] for tile in range(ref.shape[0])]
    return jnp.concatenate(parts, axis=1)


def radial_rows(first, hid_ref, out_ref, radial_ref):
    def step(g, carry):
        radial_ref[g] = dot(hid_ref[first + g], out_ref[...])
        return carry

    lax.fori_loop(0, radial_ref.shape[0], step, 0, unroll=4)


def geometry_kernel(
    vec_ref, count_ref, index_ref, y_ref, phi_ref, where_ref
):
    slots, atoms = index_ref.shape
    live = lax.broadcasted_iota(jnp.int32, (slots, atoms), 0) < count_ref[...]
    weight = by_group(jnp.where(live, 0.25, 0.0))
    vx, vy, vz = (by_group(vec_ref[n]) for n in range(3))
    rows, radius, inverse = harmonics(vx, vy, vz, weight)
    coarse = [row.astype(BF16).astype(F32) for row in rows]
    store_rows(y_ref, coarse + [row - near for row, near in zip(rows, coarse)])
    store_rows(phi_ref, radial_basis(radius, inverse, 5.0))
    where_ref[...] = by_group(index_ref[...].astype(F32)).astype(jnp.int32)


def first_radial_kernel(
    in1_ref, in2_ref, out1_ref, out2_ref, emb_ref, msg_ref, phi_ref,
    hid_ref, rows_ref, wide1_ref, wide2_ref, radial_ref,
):
    rows_ref[...] = dot(emb_ref[...], msg_ref[...]).astype(BF16)
    empty = jnp.zeros((64, 512), BF16)
    wide1_ref[:64, :], wide1_ref[64:, :] = out1_ref[...], empty
    wide2_ref[:64, :], wide2_ref[64:, :] = empty, out2_ref[...]
    groups = hid_ref.shape[0]
    into = jnp.concatenate([in1_ref[...], in2_ref[...]], axis=1)
    for g in range(groups):
        value = dot_first(basis_rows(phi_ref, g, groups).astype(BF16), into)
        hid_ref[g] = (value / (1.0 + jnp.exp(-value))).astype(BF16)
    radial_rows(0, hid_ref, wide1_ref, radial_ref)


def radial_kernel(first):
    def kernel(hid_ref, out_ref, radial_ref):
        radial_rows(first, hid_ref, out_ref, radial_ref)

    return kernel


def last_radial_kernel(first):
    def kernel(hid_ref, out_ref, dec_ref, radial_ref, blocks_ref):
        radial_rows(first, hid_ref, out_ref, radial_ref)
        column = lax.broadcasted_iota(jnp.int32, (8, 128), 1)
        repeat = (column & 7) == lax.broadcasted_iota(jnp.int32, (8, 128), 0)
        repeat = jnp.where(repeat, 1.0, 0.0).astype(BF16)
        group = lax.broadcasted_iota(jnp.int32, (128, 128), 1) >> 3
        for degree in range(4):
            wide = dot_first(dec_ref[degree], repeat)
            for m in range(degree * degree, (degree + 1) * (degree + 1)):
                block = jnp.where(group == m, wide, 0.0).astype(BF16)
                blocks_ref[m * 128 : (m + 1) * 128, :] = block

    return kernel


def group_sums(g, groups, radial, y_ref, picked):
    own = (lax.broadcasted_iota(jnp.int32, (8, 256), 1) & 7) == lax.broadcasted_iota(
        jnp.int32, (8, 256), 0
    )
    twice = jnp.concatenate([picked, picked], axis=1)
    sums = []
    for degrees, first, last in (((0, 1), 0, 4), ((2, 3), 4, 16)):
        lane = degrees[0] * 128
        weighted = (radial[:, lane : lane + 256] * twice).astype(BF16)
        angular = [
            jnp.where(own, spread(y_ref, (m + part) * groups + g), 0.0)
            for part in (0, 16)
            for m in range(first, last)
        ]
        total = dot(jnp.concatenate(angular, axis=0).astype(BF16), weighted)
        total = total[: 8 * (last - first)] + total[8 * (last - first) :]
        for m in range(first, last):
            side = 0 if m < (degrees[0] + 1) ** 2 else 128
            sums.append(total[8 * (m - first) : 8 * (m - first + 1), side : side + 128])
    return sums


def each_pair(radials, pair):
    first = 0
    for radial in radials:

        def step(j, carry, first=first, radial=radial):
            groups = [(first + 2 * j + n, radial.at[2 * j + n]) for n in range(2)]
            pair(pl.multiple_of((first + 2 * j) * 8, 16), groups)
            return carry

        lax.fori_loop(0, radial.shape[0] // 2, step, 0, unroll=4)
        first += radial.shape[0]


def layer_one_kernel(
    species_ref, xl, xh, yl, yh, zl, zh, where_ref, y_ref, radial_a, radial_b, rows_ref, emb_ref,
    self_ref, mix_ref, msg2_ref, lists_ref, next_ref, low_ref, high_ref, onehot, feats,
):
    groups, edges = where_ref.shape
    atoms = species_ref.shape[1]
    table = species_rows(species_ref, (xl, xh, yl, yh, zl, zh))
    blocks = []
    for lane in range(0, edges, 128):
        column = []
        for row in range(0, groups, 8):
            where = swapped(where_ref[row : row + 8, lane : lane + 128])
            found = jnp.zeros((8, 128), F32)
            for b in range(5):
                part = jnp.take_along_axis(table[:, b * 128 : (b + 1) * 128], where & 127, axis=1)
                found = jnp.where((where >> 7) == b, part, found)
            column.append(found)
        blocks.append(jnp.concatenate(column, axis=0))
    kinds = jnp.concatenate(blocks, axis=1).T.astype(BF16)
    lane_group = lax.broadcasted_iota(jnp.int32, (groups, 8 * groups), 1) >> 3
    widen = lane_group == lax.broadcasted_iota(jnp.int32, (groups, 8 * groups), 0)
    kinds = dot(kinds, jnp.where(widen, 1.0, 0.0).astype(BF16))
    kind_of_lane = lax.broadcasted_iota(jnp.int32, kinds.shape, 1) & 7
    onehot[...] = jnp.where(kinds == kind_of_lane.astype(F32), 1.0, 0.0).astype(BF16)
    tall = jnp.concatenate([rows_ref[...].astype(F32)] * groups, axis=0)
    row_group = lax.broadcasted_iota(jnp.int32, tall.shape, 0) >> 3

    def pair(row, members):
        parts = []
        own_rows = [jnp.where(row_group == g, tall, 0.0) for g, _ in members]
        found = dot(onehot[...], jnp.concatenate(own_rows, axis=1).astype(BF16))
        for n, (g, radial) in enumerate(members):
            sums = group_sums(g, groups, radial, y_ref, found[:, 128 * n : 128 * (n + 1)])
            part = [sums[0]]
            for degree in (1, 2, 3):
                part.append(sum(v * v for v in sums[degree * degree : (degree + 1) ** 2]))
            parts.append(jnp.concatenate(part, axis=1))
        feats[pl.ds(row, 16), :] = jnp.concatenate(parts, axis=0).astype(BF16)

    each_pair((radial_a, radial_b), pair)
    kind_ids = lax.broadcasted_iota(jnp.int32, (8, atoms), 0).astype(F32)
    own = jnp.where(table[:, :atoms] == kind_ids, 1.0, 0.0).astype(BF16)
    start = dot_first(own, emb_ref[...]).astype(BF16)
    mixed = dot(start, self_ref[...]) + dot(feats[...], mix_ref[...])
    hidden = (mixed / (1.0 + jnp.exp(-mixed))).astype(BF16)
    message = dot(hidden, msg2_ref[...]).astype(BF16)
    next_ref[...] = message
    send_rows(lists_ref, 0, message, low_ref, high_ref)


def layer_two_kernel(
    own_ref, xl, xh, yl, yh, zl, zh, where_ref, y_ref, radial_a, radial_b, radial_c, blocks_ref,
    lists_ref, coeff_ref, low_ref, high_ref, feats, wide, index,
):
    groups, edges = where_ref.shape
    pieces = [piece[...].astype(F32) for piece in (own_ref, xl, xh, yl, yh, zl, zh)]
    table = jnp.concatenate(pieces + [jnp.zeros((128, 128), F32)], axis=0)
    table = jnp.concatenate([table[256 * n : 256 * (n + 1)] for n in range(3)], axis=1)
    wide[...] = table[:, :384].astype(BF16)
    halves = (where_ref[...] & 255, where_ref[...] >> 8)
    index[...] = jnp.concatenate([half.astype(F32).T for half in halves], axis=1).astype(BF16)
    source = lax.broadcasted_iota(jnp.int32, (2 * groups, 512), 0)
    target = lax.broadcasted_iota(jnp.int32, (2 * groups, 512), 1) >> 7
    low_ids = lax.broadcasted_iota(jnp.int32, (edges, 128), 1).astype(F32)

    def pair(row, members):
        parts, onehots = [], []
        first = members[0][0]
        picks = source == first + (target & 1) + jnp.where(target < 2, 0, groups)
        spread_index = dot(index[...], jnp.where(picks, 1.0, 0.0).astype(BF16))
        for n in range(2):
            low = spread_index[:, 128 * n : 128 * (n + 1)]
            sides = [jnp.where(low == low_ids + 128.0 * side, 1.0, 0.0) for side in range(2)]
            onehots.append(jnp.concatenate(sides, axis=1))
        found = dot(jnp.concatenate(onehots, axis=0).astype(BF16), wide[...])
        for n, (g, radial) in enumerate(members):
            high = spread_index[:, 256 + 128 * n : 384 + 128 * n]
            mine = found[edges * n : edges * (n + 1)]
            picked = jnp.where(high < 0.5, mine[:, :128], mine[:, 128:256])
            picked = jnp.where(high < 1.5, picked, mine[:, 256:])
            sums = group_sums(g, groups, radial, y_ref, picked)
            parts.append(jnp.concatenate(sums, axis=1))
        feats[pl.ds(row, 16), :] = jnp.concatenate(parts, axis=0).astype(BF16)

    each_pair((radial_a, radial_b, radial_c), pair)
    coeffs = dot(feats[...], blocks_ref[...]).astype(BF16)
    coeff_ref[...] = coeffs
    send_rows(lists_ref, 0, coeffs, low_ref, high_ref)


SWAPS = ((2, 1), (1, 1), (2, 0), (1, 0))


def partner_slot(distance, first):
    ahead = (lax.axis_index("gy") // distance) % 2 == first
    return jnp.where(ahead, 2 + distance, 2 - distance)


def brick_kernel(list_ref, *rest):
    pieces, outs, chosen = rest[:7], rest[7:12], rest[12]
    table = jnp.concatenate([piece[...] for piece in pieces], axis=0)
    chosen[...] = dot_first(onehot_of(list_ref[...], table.shape[0]), table)
    for swap, out in zip(SWAPS, outs):
        first = pl.multiple_of(partner_slot(*swap) * 32, 32)
        out[...] = chosen[pl.ds(first, 32), :].astype(BF16)
    outs[4][...] = chosen[64:96].astype(BF16)


def probe_kernel(
    column, list_ref, count_ref, vec_ref, index_ref, y_ref, phi_ref, where_ref, nearby_ref
):
    slots, probes = index_ref.shape
    live = lax.broadcasted_iota(jnp.int32, (slots, probes), 0) < count_ref[...]
    weight = jnp.where(live, 0.125, 0.0)
    rows, radius, inverse = harmonics(vec_ref[0], vec_ref[1], vec_ref[2], weight)
    store_rows(y_ref, rows)
    store_rows(phi_ref, radial_basis(radius, inverse, 4.0))
    here = lax.axis_index("gy")
    index = index_ref[...]
    source = (index >> 5) - here + 2
    source = jnp.where(source < 0, source + column, source)
    source = jnp.where(source >= column, source - column, source)
    where_ref[...] = source * 32 + (index & 31)
    targets = list_ref.shape[1]
    start = (2 - here) * (targets // column)
    start = jnp.where(start < 0, start + targets, start)
    turned = pltpu.roll(jnp.broadcast_to(list_ref[...], (8, targets)), start, axis=1)
    nearby_ref[...] = turned[:1, :256]


def probe_onehot_kernel(where_ref, onehot_ref):
    def step(k, carry):
        onehot_ref[k] = onehot_of(where_ref[pl.ds(k, 1), :], onehot_ref.shape[1])
        return carry

    lax.fori_loop(0, where_ref.shape[0], step, 0, unroll=2)


def density_kernel(p0, p1, p2, p3, p4, onehot_ref, y, phi, out_ref, table):
    slots, _, probes = onehot_ref.shape
    table[160:, :] = jnp.zeros((96, 128), F32)
    table[64:96, :] = p4[...].astype(F32)
    for swap, piece in zip(SWAPS, (p0, p1, p2, p3)):
        first = pl.multiple_of(partner_slot(*swap) * 32, 32)
        table[pl.ds(first, 32), :] = piece[...].astype(F32)
    rows_t = table[...].T[:, :160].astype(BF16)

    def slot(k, total):
        picked = dot(rows_t, onehot_ref[k])
        part = jnp.zeros((8, probes), F32)
        for m in range(16):
            part = part + spread(y, m * slots + k) * picked[m * 8 : (m + 1) * 8]
        return total + part * basis_rows(phi, k, slots)

    total = lax.fori_loop(0, slots, slot, jnp.zeros((8, probes), F32), unroll=4)
    out_ref[...] = jnp.sum(total, axis=0, keepdims=True)


def shifted(block, axis, step):
    size = lax.axis_size(axis)
    return lax.ppermute(block, axis, [(i, (i + step) % size) for i in range(size)])


def swapped_with(block, distance, first):
    size = lax.axis_size("gy")
    pairs = []
    for low in range(size):
        if (low // distance) % 2 == first:
            high = (low + distance) % size
            pairs += [(low, high), (high, low)]
    return lax.ppermute(block, "gy", sorted(pairs))


def extend(rows, low, high, lists, fillers):
    half = jax.ShapeDtypeStruct((64, 128), BF16)
    pieces, made, begin = [], [], rows
    for section, axis in enumerate(("gx", "gy", "gz")):
        if section:
            done = made[-1][-1:] if made[-1] else ()
            low, high = call(
                pick_rows(section), (half, half), (lists, rows, *pieces), after=done
            )
            begin = low
        pieces += [shifted(low, axis, 1), shifted(high, axis, -1)]
        made.append(fillers[section](made, begin) if fillers[section] else ())
    return pieces, made


def shards(
    species, neighbour_index, neighbour_count, edge_vectors, ghost_send, brick_send, probe_index,
    probe_count, probe_vectors, embedding, message_one, radial_in_one, radial_out_one, self_mix,
    basis_mix, message_two, radial_in_two, radial_out_two, decoder,
):
    slots, atoms = neighbour_index.shape[3:]
    probes = probe_index.shape[-1]
    kinds = species.reshape(1, atoms)
    lists = ghost_send.reshape(1, 384)
    shape = jax.ShapeDtypeStruct
    half = shape((64, 128), BF16)
    column = lax.axis_size("gy")

    def both(block, axis):
        return [shifted(block, axis, 1), shifted(block, axis, -1)]

    row = shape((8, 128), F32)
    hidden = shape((slots, atoms, 128), BF16)
    wide = shape((128, 512), BF16)

    def radial(count):
        return shape((count, atoms, 512), F32)

    chosen, kinds, lists = call(
        first_kernel,
        (row, shape(kinds.shape, jnp.int32), shape(lists.shape, jnp.int32)),
        (),
        staged=(kinds, lists),
    )
    ghosts = both(chosen, "gx")
    angular, phi, where = call(
        geometry_kernel,
        (
            shape((2, 32 * slots, 128), F32),
            shape((2, BASIS * slots, 128), F32),
            shape((slots, atoms), jnp.int32),
        ),
        (),
        staged=(
            edge_vectors.reshape(3, slots, atoms),
            neighbour_count.reshape(1, atoms),
            neighbour_index.reshape(slots, atoms),
        ),
        after=(chosen,),
    )
    chosen = call(pick_species(1), row, (kinds, lists, *ghosts), after=(where,))
    ghosts += both(chosen, "gy")
    hidden_both, rows, wide_one, wide_two, radial_a = call(
        first_radial_kernel,
        (hidden, shape((8, 128), BF16), wide, wide, radial(8)),
        (phi,),
        limit=20,
        staged=(
            radial_in_one,
            radial_in_two,
            radial_out_one,
            radial_out_two,
            embedding,
            message_one,
        ),
        after=(chosen,),
    )
    chosen = call(pick_species(2), row, (kinds, lists, *ghosts), after=(radial_a,))
    ghosts += both(chosen, "gz")
    radial_b = call(
        radial_kernel(8), radial(24), (hidden_both, wide_one), limit=30, after=(chosen,)
    )
    second = call(
        layer_one_kernel,
        (shape((atoms, 128), BF16), half, half),
        (kinds, *ghosts, where, angular, radial_a, radial_b, rows, embedding, self_mix,
         basis_mix, message_two, lists),
        [pltpu.VMEM((atoms, 256), BF16), pltpu.VMEM((atoms, 512), BF16)],
        limit=16,
    )
    pieces, made = extend(
        *second,
        lists,
        (
            lambda made, begin: (
                call(
                    radial_kernel(0),
                    radial(8),
                    (hidden_both, wide_two),
                    limit=20,
                    after=(begin,),
                ),
            ),
            lambda made, begin: (
                call(
                    radial_kernel(8),
                    radial(16),
                    (hidden_both, wide_two),
                    limit=20,
                    after=(begin,),
                ),
            ),
            lambda made, begin: call(
                last_radial_kernel(24),
                (radial(8), shape((2048, 128), BF16)),
                (hidden_both, wide_two, decoder.transpose(0, 2, 1)),
                limit=20,
                after=(begin,),
            ),
        ),
    )
    coeffs = call(
        layer_two_kernel,
        (shape((atoms, 128), BF16), half, half),
        (second[0], *pieces, where, angular, made[0][0], made[1][0], *made[2], lists),
        [
            pltpu.VMEM((atoms, 2048), BF16),
            pltpu.VMEM((256, 384), BF16),
            pltpu.VMEM((atoms, 2 * slots), BF16),
        ],
        limit=16,
    )
    pieces, made = extend(
        *coeffs,
        lists,
        (
            lambda made, begin: call(
                functools.partial(probe_kernel, column),
                (
                    shape((probes // 128, 16 * slots, 128), F32),
                    shape((probes // 128, BASIS * slots, 128), F32),
                    shape((slots, probes), jnp.int32),
                    shape((1, 256), jnp.int32),
                ),
                (
                    brick_send.reshape(1, -1),
                    probe_count.reshape(1, probes),
                    probe_vectors.reshape(3, slots, probes),
                    probe_index.reshape(slots, probes),
                ),
                after=(begin,),
            ),
            lambda made, begin: (
                call(
                    probe_onehot_kernel,
                    shape((slots, 160, probes), BF16),
                    (made[0][2],),
                    limit=12,
                    after=(begin,),
                ),
            ),
            None,
        ),
    )
    probe_y, probe_phi, _, nearby = made[0]
    sent = call(
        brick_kernel,
        [shape((32, 128), BF16)] * 5,
        (nearby, coeffs[0], *pieces),
        [pltpu.VMEM((256, 128), F32)],
    )
    pieces = [swapped_with(sent[n], *SWAPS[n]) for n in (3, 2, 1, 0)][::-1] + [sent[4]]
    density = call(
        density_kernel,
        shape((1, probes), F32),
        (*pieces, made[1][0], probe_y, probe_phi),
        [pltpu.VMEM((256, 128), F32)],
        limit=16,
    )
    return density.reshape(1, 1, 1, probes)


def solution(mesh):
    domain = ("gx", "gy", "gz")
    placed = tuple(P(*domain) for _ in range(9)) + tuple(P() for _ in range(10))
    return jax.shard_map(
        shards, mesh=mesh, in_specs=placed, out_specs=P(*domain), check_vma=False
    )
```
